32 devices in a mesh: space: 16 (over z, y, x), coil: 2 (over core).
Axes of the slice: x: 2, y: 2, z: 4, core: 2. Of those that a mesh axis runs over, the one named last changes fastest.
Arguments:
- state: bfloat16 [32, 2, 1024, 768], P(None, None, 'space', 'coil'), may hold values from -6 to 6
- sens: float32 [2, 16, 2, 1024, 768], P(None, 'coil', None, 'space'), may hold values from -2 to 2
- kdata: float32 [2, 16, 2, 768, 1024], P(None, 'coil', None, 'space'), may hold values from -3 to 3
- mask: int32 [768, 1024], P('space'), may hold values 0 or 1
- inject: float32 [32, 2], replicated, may hold values from -4 to 4
- kernels: bfloat16 [4, 27, 16, 16], replicated, may hold values from -0.3125 to 0.3125
- biases: float32 [4, 16], replicated, may hold values from -3 to 3
- mixers: bfloat16 [4, 16, 16], replicated, may hold values from -1.5 to 1.5
Outputs:
- new_state: bfloat16 [32, 2, 1024, 768], P(None, None, 'space', 'coil')
- gradient: float32 [2, 2, 1024, 768], P(None, None, 'space', 'coil')
The draws below stay inside these ranges and needn't reach their ends.
All inputs are finite; a program needn't handle non-finite values. No bound on the sum of `mask` on one device may be relied on, other than what follows from the above.
Results may differ from the reference program's by a relative error of at most 0.015.
Values may be sent and summed in bfloat16 or wider, within the bound.
A program may use at most 128 MiB of HBM per device.

```python
import jax
import jax.numpy as jnp
from jax import lax

NPE = 1024
NPAR = 768
COILS = 16
CH = 32
POS = 2
COUPLINGS = 4


def with_ends(result, key, smallest, largest):
    index_at = [jax.random.randint(jax.random.fold_in(key, axis), (), 0, length) for axis, length in enumerate(result.shape)]
    widest = result.shape.index(max(result.shape))
    neighbour = index_at[:widest] + [(index_at[widest] + 1) % result.shape[widest]] + index_at[widest + 1:]
    return result.at[tuple(index_at)].set(smallest).at[tuple(neighbour)].set(largest)


def steps_of(stream_key, dims, cuts, least, largest):
    loudness = 1.0
    for dim, blocks in cuts:
        steps = jax.random.uniform(jax.random.fold_in(jax.random.fold_in(stream_key, 6), dim), (blocks,), jnp.float32, least / len(cuts), largest / len(cuts))
        loudness = loudness * jnp.repeat(jnp.exp(steps), dims[dim] // blocks).reshape((-1,) + (1,) * (len(dims) - 1 - dim))
    return loudness


def normal_values(key, dims, scale, reach, cuts=(), held_as=jnp.bfloat16):
    values = scale * jax.random.normal(key, dims, jnp.float32)
    if cuts:
        values = values * steps_of(key, dims, cuts, -0.22, 0.18)
    return jnp.clip(values, -reach, reach).astype(held_as)


def setup_inputs(seed: int = 0) -> dict:
    key_of = jax.random.split(jax.random.key(seed), 9)
    state = normal_values(key_of[0], (CH, POS, NPE, NPAR), 1.0, 6.0, ((2, 16), (3, 2)))
    sens = normal_values(key_of[1], (2, COILS, POS, NPE, NPAR), 0.25, 2.0, ((1, 2), (3, 16)), jnp.float32)
    kdata = normal_values(key_of[2], (2, COILS, POS, NPAR, NPE), 0.35, 3.0, ((1, 2), (3, 16)), jnp.float32)
    mask = with_ends((jax.random.randint(key_of[3], (NPAR, NPE), 0, 3) < 1).astype(jnp.int32), jax.random.fold_in(key_of[3], 1), 0, 1)
    inject = normal_values(key_of[4], (CH, 2), 2 ** -0.5, 4.0, (), jnp.float32)
    kernels = normal_values(key_of[5], (COUPLINGS, 27, CH // 2, CH // 2), (27 * (CH // 2)) ** -0.5, 0.3125)
    biases = normal_values(key_of[6], (COUPLINGS, CH // 2), 0.5, 3.0, (), jnp.float32)
    mixers = normal_values(key_of[7], (COUPLINGS, CH // 2, CH // 2), (CH // 2) ** -0.5, 1.5)
    return dict(state=state, sens=sens, kdata=kdata, mask=mask, inject=inject, kernels=kernels, biases=biases, mixers=mixers)


def coupling(source, target, kernel, bias, mixer):
    weight = jnp.transpose(kernel.astype(jnp.float32).reshape(3, 3, 3, kernel.shape[1], kernel.shape[2]), (3, 4, 0, 1, 2))
    raw = lax.conv_general_dilated(source.astype(jnp.float32)[None], weight, (1, 1, 1), "SAME", dimension_numbers=("NCDHW", "OIDHW", "NCDHW"), precision=lax.Precision.HIGHEST)[0]
    hidden = jax.nn.relu(raw + bias[:, None, None, None]).astype(jnp.bfloat16)
    mixed = jnp.einsum("oi,ipqr->opqr", mixer.astype(jnp.float32), hidden.astype(jnp.float32), precision=lax.Precision.HIGHEST)
    return (target.astype(jnp.float32) + mixed).astype(jnp.bfloat16)


def reference(state, sens, kdata, mask, inject, kernels, biases, mixers):
    estimate = state[0].astype(jnp.float32) + 1j * state[1].astype(jnp.float32)
    weight = mask.astype(jnp.float32)

    def one_coil(total, pieces):
        sens_real, sens_imag, data_real, data_imag = pieces
        profile = sens_real + 1j * sens_imag
        spectrum = jnp.fft.fft2(profile * estimate, axes=(-2, -1), norm="ortho")
        spectrum = jnp.swapaxes(spectrum, -1, -2)
        residual = weight * (spectrum - (data_real + 1j * data_imag))
        image = jnp.fft.ifft2(jnp.swapaxes(residual, -1, -2), axes=(-2, -1), norm="ortho")
        term = jnp.conj(profile) * image
        return total + jnp.stack([jnp.real(term), jnp.imag(term)]).astype(jnp.float32), None

    start = jnp.zeros((2, POS, NPE, NPAR), jnp.float32)
    gradient, _ = lax.scan(one_coil, start, (sens[0], sens[1], kdata[0], kdata[1]))
    added = jnp.einsum("cg,gpqr->cpqr", inject, gradient, precision=lax.Precision.HIGHEST)
    merged = (state.astype(jnp.float32) + added).astype(jnp.bfloat16)
    half = CH // 2
    first = merged[:half]
    second = merged[half:]
    for layer in range(COUPLINGS):
        if layer % 2 == 0:
            second = coupling(first, second, kernels[layer], biases[layer], mixers[layer])
        else:
            first = coupling(second, first, kernels[layer], biases[layer], mixers[layer])
    new_state = jnp.concatenate([first, second], axis=0)
    return new_state, gradient
```

```python
import functools
import math

import jax
import jax.numpy as jnp
import numpy as np
from jax import lax
from jax.experimental import pallas as pl
from jax.experimental.pallas import tpu as pltpu
from jax.sharding import PartitionSpec as P

HALO = 4
BLOCK = 6
GROUP = 16
f32, bf16 = jnp.float32, jnp.bfloat16


def dft_table(length):
    turns = np.arange(length)[:, None] * np.arange(length)[None, :] % length * (2.0 * math.pi / length)
    table = np.stack([np.cos(turns), np.sin(turns)]) / math.sqrt(length)
    return jnp.asarray(table.astype(np.float32).astype(bf16))


def row_chunks(rows):
    sizes = [rows // 2] if rows % (2 * GROUP) == 0 else []
    while sum(sizes) < rows:
        sizes.append(min(GROUP, rows - sum(sizes)))
    starts = [sum(sizes[:k]) for k in range(len(sizes))]
    return list(zip(starts, sizes))


def packed(positions, size, count):
    group = max(1, 128 // (2 * positions * size))
    while count % group:
        group -= 1
    return group


def column(row, length):
    ones = lax.broadcasted_iota(jnp.int32, (length, length), 0) == lax.broadcasted_iota(jnp.int32, (length, length), 1)
    return jnp.sum(jnp.where(ones, jnp.broadcast_to(row, (length, length)), 0.0), axis=1, keepdims=True)


def swapped(outer, inner):
    size = outer * inner
    to = lax.broadcasted_iota(jnp.int32, (size, size), 0)
    of = lax.broadcasted_iota(jnp.int32, (size, size), 1)
    same = (to // inner == of % outer) & (to % inner == of // outer)
    return jnp.where(same, 1.0, 0.0).astype(bf16)


def body(dims, state_hbm, sens_hbm, kdata_hbm, par_hbm, pe_hbm, mask_ref, inject_ref, kernel_ref, bias_ref, mixer_ref,
         state_out, gradient_out,
         sens_ref, kdata_ref, state_ref, par_ref, pe_ref,
         seen, whole, send_out, got_out, send_back, got_back, total, part, parts, edge, edges,
         halves, strips, borders, weight, strip, mix, bias, spread, inward, outward, stage, summed,
         sens_in, kdata_in, state_in, par_in, pe_in, est_in, stage_out, summed_out,
         seen_sent, seen_got, out_sent, out_got, back_sent, back_got, part_sent, part_got, edge_sent, edge_got,
         row_sent, row_got, col_sent, col_got):
    spaces, coils, total_rows, total_cols, chunks = dims
    mesh_id = pl.DeviceIdType.MESH
    space = lax.axis_index("space")
    coil = lax.axis_index("coil")
    channels, positions, rows, width = state_ref.shape
    half_of = channels // 2
    unit = positions * half_of
    layers = kernel_ref.shape[0]
    count, npar = sens_ref.shape[1], sens_ref.shape[4]
    held, npe = kdata_ref.shape[3:]
    lanes = halves.shape[3]
    deep = halves.shape[1]
    sites = positions * rows
    lines = positions * held
    has_above, has_below = space > 0, space < spaces - 1
    has_left, has_right = coil > 0, coil < coils - 1

    def turn(value, step, size):
        return lax.rem(value + step + size, size)

    fetch_par = pltpu.make_async_copy(par_hbm, par_ref, par_in)
    fetch_pe = pltpu.make_async_copy(pe_hbm, pe_ref, pe_in)
    fetch_kdata = pltpu.make_async_copy(kdata_hbm, kdata_ref, kdata_in)
    fetch_state = pltpu.make_async_copy(state_hbm, state_ref, state_in)
    fetch_estimate = pltpu.make_async_copy(state_hbm.at[0:2], seen.at[coil], est_in)

    def fetch_sens(c):
        return pltpu.make_async_copy(sens_hbm.at[:, c], sens_ref.at[:, c], sens_in.at[c])

    fetch_estimate.start()
    fetch_state.start()
    fetch_par.start()

    @pl.loop(0, count)
    def _(c):
        fetch_sens(c).start()

    fetch_pe.start()
    fetch_kdata.start()

    barrier = pltpu.get_barrier_semaphore()

    @pl.loop(1, spaces)
    def _(offset):
        pl.semaphore_signal(barrier, inc=1, device_id={"space": lax.rem(space + offset, spaces)}, device_id_type=mesh_id)

    for offset in range(1, coils):
        other = lax.rem(coil + offset, coils)
        pl.semaphore_signal(barrier, inc=1, device_id={"coil": other}, device_id_type=mesh_id)
        for step in (1, -1):
            pl.semaphore_signal(barrier, inc=1, device_id={"space": turn(space, step, spaces), "coil": other},
                                device_id_type=mesh_id)
    pl.semaphore_wait(barrier, spaces - 1 + 3 * (coils - 1))

    def to_coil(source, target, offset, sent, got):
        return pltpu.make_async_remote_copy(
            src_ref=source, dst_ref=target, send_sem=sent.at[offset], recv_sem=got.at[offset],
            device_id={"coil": lax.rem(coil + offset, coils)}, device_id_type=mesh_id)

    def to_space(buffer, target, c, offset, sent, got):
        other = lax.rem(space + offset, spaces)
        return pltpu.make_async_remote_copy(
            src_ref=buffer.at[c, other], dst_ref=target.at[c, space], send_sem=sent.at[c], recv_sem=got.at[c],
            device_id={"space": other}, device_id_type=mesh_id)

    def send_all(buffer, target, c, sent, got):
        @pl.loop(1, spaces)
        def _(offset):
            to_space(buffer, target, c, offset, sent, got).start()

    def all_of(buffer, c, sem):
        span = buffer.at[c, pl.ds(0, spaces - 1)]
        pltpu.make_async_copy(span, span, sem.at[c]).wait()

    for offset in range(1, coils):
        to_coil(state_hbm.at[0:2], seen.at[coil], offset, seen_sent, seen_got).start()

    inward[...] = swapped(GROUP, half_of)
    outward[...] = swapped(half_of, GROUP)

    def clear(row, many):
        for half in range(2):
            halves[half, pl.ds(row, many)] = jnp.zeros((many, unit, lanes), bf16)

    def row_major(g):
        at = pl.ds(pl.multiple_of(g * GROUP, GROUP), GROUP)
        into = pl.ds(g * GROUP + HALO, GROUP)
        for half in range(2):
            for p in range(positions):
                cells = state_ref[half * half_of:(half + 1) * half_of, p, at, :].reshape(half_of * GROUP, width)
                moved = jnp.dot(inward[...], cells, preferred_element_type=f32)
                moved = moved.reshape(GROUP, half_of, width).astype(bf16)
                if lanes > width:
                    moved = jnp.concatenate([moved, jnp.zeros((GROUP, half_of, lanes - width), bf16)], axis=-1)
                halves[half, into, p * half_of:(p + 1) * half_of, :] = moved

    def upright(way):
        source, target = (rows, HALO)[way], (0, HALO + rows)[way]
        return pltpu.make_async_remote_copy(
            src_ref=halves.at[:, pl.ds(source, HALO), :, pl.ds(0, wide)],
            dst_ref=halves.at[:, pl.ds(target, HALO), :, pl.ds(0, wide)],
            send_sem=row_sent.at[way], recv_sem=row_got.at[way],
            device_id={"space": turn(space, (1, -1)[way], spaces)}, device_id_type=mesh_id)

    wide = -(-width // 128) * 128
    groups = rows // GROUP
    fetch_state.wait()

    @pl.when(space == 0)
    def _():
        clear(0, HALO)

    @pl.when(space == spaces - 1)
    def _():
        clear(HALO + rows, HALO)

    if wide < lanes:
        for first in (0, HALO + rows):
            halves[:, pl.ds(first, HALO), :, wide:lanes] = jnp.zeros((2, HALO, unit, lanes - wide), bf16)
    row_major(0)

    @pl.when(has_above)
    def _():
        upright(1).start()

    if groups > 1:
        row_major(groups - 1)

    @pl.when(has_below)
    def _():
        upright(0).start()

    fetch_estimate.wait()
    fetch_par.wait()
    for offset in range(1, coils):
        to_coil(state_hbm.at[0:2], seen.at[coil], offset, seen_sent, seen_got).wait()
    for k in range(2):
        whole[k] = jnp.concatenate([seen[j, k].astype(f32).reshape(sites, width) for j in range(coils)], axis=-1)

    @pl.loop(0, count)
    def _(c):
        fetch_sens(c).wait()
        profile_real = sens_ref[0, c].reshape(sites, npar)
        profile_imag = sens_ref[1, c].reshape(sites, npar)
        real = profile_real * whole[0] - profile_imag * whole[1]
        imag = profile_real * whole[1] + profile_imag * whole[0]
        plain = jnp.concatenate([real, imag], axis=0).astype(bf16)
        turned = jnp.concatenate([imag, -real], axis=0).astype(bf16)
        along = (((1,), (1,)), ((), ()))
        spectrum = lax.dot_general(par_ref[0], plain, along, preferred_element_type=f32)
        spectrum += lax.dot_general(par_ref[1], turned, along, preferred_element_type=f32)
        send_out[c] = spectrum.reshape(spaces, held, 2 * sites).astype(bf16)
        send_all(send_out, got_out, c, out_sent, out_got)
        got_out[c, space] = send_out[c, space]

    if groups > 2:
        @pl.loop(1, groups - 1)
        def _(g):
            row_major(g)

    clear(rows + 2 * HALO, deep - rows - 2 * HALO)

    @pl.loop(0, layers)
    def _(k):
        bands = unit * (BLOCK + 2)
        strip[...] = jnp.zeros_like(strip)
        for a in range(3):
            for po in range(positions):
                pi = po + a - 1
                if 0 <= pi < positions:
                    for b in range(3):
                        for c in range(3):
                            at = b * unit + pi * half_of
                            tap = kernel_ref[k, 9 * a + 3 * b + c].astype(f32)
                            strip[c, po * half_of:(po + 1) * half_of, at:at + half_of] = tap
        for c in range(3):
            for x in range(BLOCK):
                line = pltpu.roll(strip[c], unit * x, 1) if x else strip[c]
                weight[k, c, unit * x:unit * (x + 1), :] = line[:, :bands].astype(bf16)
        own = mixer_ref[k].astype(f32)
        times = positions * BLOCK
        for x in range(times):
            parts_of = [jnp.zeros((half_of, half_of * x), f32)] if x else []
            parts_of.append(own)
            if x < times - 1:
                parts_of.append(jnp.zeros((half_of, half_of * (times - 1 - x)), f32))
            mix[k, half_of * x:half_of * (x + 1), :] = jnp.concatenate(parts_of, axis=-1).astype(bf16)
        offsets = column(bias_ref[pl.ds(k, 1), :], half_of)
        bias[k] = jnp.concatenate([jnp.broadcast_to(offsets, (half_of, 128))] * times, axis=0)

    for half in range(2):
        for g in range(2):
            gains = column(inject_ref[g:g + 1, half * half_of:(half + 1) * half_of], half_of)
            spread[half, g] = jnp.concatenate([jnp.broadcast_to(gains, (half_of, 128))] * positions, axis=0)

    @pl.when(has_below)
    def _():
        upright(0).wait_send()
        upright(1).wait_recv()

    @pl.when(has_above)
    def _():
        upright(1).wait_send()
        upright(0).wait_recv()

    lane = lax.broadcasted_iota(jnp.int32, (1, lanes), 1)

    @pl.loop(0, rows + 2 * HALO)
    def _(row):
        for half in range(2):
            line = jnp.where(lane < width, halves[half, row].astype(f32), 0.0)
            strips[0, half, row] = pltpu.roll(line, lanes - width, 1)[:, lanes - 128:].astype(bf16)
            strips[1, half, row] = pltpu.roll(line, width, 1)[:, lanes - 128:].astype(bf16)

    def sideways(way):
        return pltpu.make_async_remote_copy(
            src_ref=strips.at[way], dst_ref=borders.at[way], send_sem=col_sent.at[way], recv_sem=col_got.at[way],
            device_id={"coil": turn(coil, (1, -1)[way], coils)}, device_id_type=mesh_id)

    @pl.when(has_right)
    def _():
        sideways(0).start()

    @pl.when(has_left)
    def _():
        sideways(1).start()

    final = lax.broadcasted_iota(jnp.int32, (1, 128), 1)

    def blend(way, inside):
        @pl.loop(0, rows + 2 * HALO)
        def _(row):
            for half in range(2):
                own = halves[half, row, :, lanes - 128:].astype(f32)
                new = borders[way, half, row].astype(f32)
                halves[half, row, :, lanes - 128:] = jnp.where(inside, new, own).astype(bf16)

    @pl.when(has_left)
    def _():
        sideways(0).wait_recv()
        blend(0, final >= 128 - HALO)

    @pl.when(has_right)
    def _():
        sideways(1).wait_recv()
        first = width % 128
        blend(1, (final >= first) & (final < first + HALO))

    @pl.when(has_right)
    def _():
        sideways(0).wait_send()

    @pl.when(has_left)
    def _():
        sideways(1).wait_send()

    fetch_pe.wait()
    fetch_kdata.wait()
    pair = max(packed(positions, size, count) for _, size in chunks)
    groups_of = [packed(positions, size, count) for _, size in chunks]

    @pl.loop(0, count // pair)
    def _(couple):
        backs = []
        for j in range(pair):
            c = couple * pair + j
            all_of(got_out, c, out_got)
            blocks = [got_out[c, s].astype(f32) for s in range(spaces)]
            grid = [
                jnp.concatenate([block[:, k * rows:(k + 1) * rows] for block in blocks], axis=-1)
                for k in range(2 * positions)
            ]
            real = jnp.concatenate(grid[:positions], axis=0)
            imag = jnp.concatenate(grid[positions:], axis=0)
            plain = jnp.concatenate([real, imag], axis=0).astype(bf16)
            turned = jnp.concatenate([imag, -real], axis=0).astype(bf16)
            full = jnp.dot(plain, pe_ref[0], preferred_element_type=f32)
            full += jnp.dot(turned, pe_ref[1], preferred_element_type=f32)
            sampled = jnp.concatenate([mask_ref[...].astype(f32)] * positions, axis=0)
            real = sampled * (full[:lines] - kdata_ref[0, c].reshape(lines, npe))
            imag = sampled * (full[lines:] - kdata_ref[1, c].reshape(lines, npe))
            plain = jnp.concatenate([real, imag], axis=0).astype(bf16)
            turned = jnp.concatenate([-imag, real], axis=0).astype(bf16)
            back = jnp.dot(plain, pe_ref[0], preferred_element_type=f32)
            back += jnp.dot(turned, pe_ref[1], preferred_element_type=f32)
            backs.append(back)
            for q, (start, size) in enumerate(chunks):
                many = groups_of[q]
                if (j + 1) % many:
                    continue
                c_group = couple * (pair // many) + j // many
                for s in range(spaces):
                    send_back[q][c_group, s] = jnp.concatenate(
                        [backs[i][k * held:(k + 1) * held, s * rows + start:s * rows + start + size]
                         for i in range(j + 1 - many, j + 1) for k in range(2 * positions)], axis=-1
                    ).astype(bf16)
                got_back[q][c_group, space] = send_back[q][c_group, space]
                if q == 0:
                    send_all(send_back[q], got_back[q], c_group, back_sent[q], back_got[q])

    def release(q):
        sets = count // groups_of[q]

        @pl.loop(0, sets)
        def _(g):
            send_all(send_back[q], got_back[q], g, back_sent[q], back_got[q])

    def drained(q, low, high):
        @pl.loop(low, high)
        def _(g):
            all_of(send_back[q], g, back_sent[q])

    column_at = jnp.where(lane >= lanes - HALO, lane - lanes, lane) + coil * width
    good = (column_at >= 0) & (column_at < total_cols) & ((lane < width + HALO) | (lane >= lanes - HALO))
    column_ok = jnp.where(good, 1.0, 0.0)
    end_ok = column_ok[:, lanes - 128:]

    def extended(value, j):
        after = min(npar, (j + 1) * width + HALO) - j * width
        before = HALO if j else 0
        room = lanes - width
        if j == 0 and lanes <= npar:
            return value[:, :lanes]
        if j == coils - 1 and j * width >= room:
            return jnp.concatenate([value[:, j * width:], value[:, j * width - room:j * width]], axis=-1)
        pieces = [value[:, j * width:j * width + after], jnp.zeros((value.shape[0], lanes - after - before), f32)]
        if before:
            pieces.append(value[:, j * width - before:j * width])
        return jnp.concatenate(pieces, axis=-1)

    def edgeways(way, j):
        return pltpu.make_async_remote_copy(
            src_ref=edge.at[way, j], dst_ref=edges.at[way, coil],
            send_sem=edge_sent.at[way, j], recv_sem=edge_got.at[way, coil],
            device_id={"space": turn(space, (1, -1)[way], spaces), "coil": j}, device_id_type=mesh_id)

    def edge_landed(way):
        for j in range(coils):
            pltpu.make_async_copy(edges.at[way, j], edges.at[way, j], edge_got.at[way, j]).wait()

    def edge_left(way):
        for j in range(coils):
            pltpu.make_async_copy(edge.at[way, j], edge.at[way, j], edge_sent.at[way, j]).wait()

    def limit(value):
        if lanes > 128:
            return jnp.concatenate([value[:, :lanes - 128], value[:, lanes - 128:] * end_ok], axis=-1)
        return value * end_ok

    def merge(row, lines_of):
        spreads = [
            jnp.concatenate([jnp.broadcast_to(lines_of[g][p], (half_of, lanes)) for p in range(positions)], axis=0)
            for g in range(2)
        ]
        for half in range(2):
            gains = [jnp.concatenate([spread[half, g]] * (lanes // 128), axis=-1) for g in range(2)]
            added = gains[0] * spreads[0] + gains[1] * spreads[1]
            halves[half, row] = (halves[half, row].astype(f32) + added).astype(bf16)

    def gradient_rows(q):
        start, size = chunks[q]
        many = groups_of[q]
        sets = count // many
        spots = positions * size
        at_once = max(1, 256 // (many * 2 * spots))
        while sets % at_once:
            at_once -= 1
        total[:, :spots] = jnp.zeros((2, spots, npar), f32)

        @pl.loop(0, sets // at_once)
        def _(step):
            plains, turneds = [], []
            for i in range(at_once):
                g = step * at_once + i
                all_of(got_back[q], g, back_got[q])
                value = got_back[q][g].astype(f32).reshape(npar, many * 2 * spots)
                plains.append(value)
                for j in range(many):
                    base = j * 2 * spots
                    turneds += [-value[:, base + spots:base + 2 * spots], value[:, base:base + spots]]
            plain = jnp.concatenate(plains, axis=-1).astype(bf16)
            turned = jnp.concatenate(turneds, axis=-1).astype(bf16)
            along = (((0,), (0,)), ((), ()))
            image = lax.dot_general(plain, par_ref[0], along, preferred_element_type=f32)
            image += lax.dot_general(turned, par_ref[1], along, preferred_element_type=f32)
            for i in range(at_once * many):
                c = step * (at_once * many) + i
                base = i * 2 * spots
                real, imag = image[base:base + spots], image[base + spots:base + 2 * spots]
                profile_real = sens_ref[0, c, :, start:start + size, :].reshape(spots, npar)
                profile_imag = sens_ref[1, c, :, start:start + size, :].reshape(spots, npar)
                total[0, :spots] += profile_real * real + profile_imag * imag
                total[1, :spots] += profile_real * imag - profile_imag * real

        for j in range(coils):
            for k in range(2):
                part[q][j, k] = extended(total[k, :spots], j).astype(bf16)
        for offset in range(1, coils):
            to_coil(part[q].at[lax.rem(coil + offset, coils)], parts[q].at[coil], offset, part_sent.at[q], part_got.at[q]).start()
        parts[q][coil] = part[q][coil]

        def put_edge(way, low):
            for j in range(coils):
                edge[way, j] = jnp.concatenate(
                    [extended(total[k, p * size + low:p * size + low + HALO], j) for k in range(2) for p in range(positions)],
                    axis=0).astype(bf16)

            @pl.when((has_below, has_above)[way])
            def _():
                for j in range(coils):
                    edgeways(way, j).start()

        if q == 0:
            put_edge(1, 0)
        if q == len(chunks) - 1:
            put_edge(0, size - HALO)
        for offset in range(1, coils):
            to_coil(part[q].at[lax.rem(coil + offset, coils)], parts[q].at[coil], offset, part_sent.at[q], part_got.at[q]).wait()
        for k in range(2):
            value = parts[q][0, k].astype(f32)
            for j in range(1, coils):
                value += parts[q][j, k].astype(f32)
            value = limit(value)
            for p in range(positions):
                summed[k, p, start:start + size, :] = value[p * size:(p + 1) * size]

        @pl.loop(start, start + size)
        def _(row):
            merge(row + HALO, [[summed[g, p, pl.ds(row, 1), :] for p in range(positions)] for g in range(2)])

    def merge_border(way):
        first = (0, HALO + rows)[way]
        edge_landed(way)
        value = edges[way, 0].astype(f32)
        for j in range(1, coils):
            value += edges[way, j].astype(f32)
        value = limit(value)
        for r in range(HALO):
            merge(first + r, [
                [value[(g * positions + p) * HALO + r:(g * positions + p) * HALO + r + 1] for p in range(positions)]
                for g in range(2)
            ])

    def cell_rows(layer, row, keep, inner):
        source, target = layer % 2, 1 - layer % 2
        cells = halves[source, pl.ds(row - 1, BLOCK + 2)].reshape((BLOCK + 2) * unit, lanes)
        raw = pltpu.roll(jnp.dot(weight[layer, 0], cells, preferred_element_type=f32), 1, 1)
        raw += jnp.dot(weight[layer, 1], cells, preferred_element_type=f32)
        raw += pltpu.roll(jnp.dot(weight[layer, 2], cells, preferred_element_type=f32), lanes - 1, 1)
        hidden = jnp.maximum(raw + jnp.concatenate([bias[layer]] * (lanes // 128), axis=-1), 0.0)
        hidden = limit(hidden)
        if not inner:
            step = lax.broadcasted_iota(jnp.int32, (BLOCK * unit, 1), 0) // unit
            at = step + (row - HALO + space * rows)
            hidden = jnp.where((at >= 0) & (at < total_rows), hidden, 0.0)
        update = jnp.dot(mix[layer], hidden.astype(bf16), preferred_element_type=f32)
        if keep < BLOCK:
            update = update[:keep * unit]
        into = pl.ds(row, keep)
        old = halves[target, into].astype(f32)
        halves[target, into] = (old + update.reshape(keep, unit, lanes)).astype(bf16)

    def cover(layer, low, high):
        many = high - low + 1
        if many <= 0:
            return
        inside = max(0, min(many, rows - low)) // BLOCK if low >= 0 else 0
        if inside:
            @pl.loop(0, inside)
            def _(b):
                cell_rows(layer, low + HALO + b * BLOCK, BLOCK, True)
        row = low + inside * BLOCK
        while row <= high:
            keep = min(BLOCK, high - row + 1)
            cell_rows(layer, row + HALO, keep, row >= 0 and row + keep <= rows)
            row += keep

    def store(g):
        return pltpu.make_async_copy(
            stage.at[g], state_out.at[:, :, pl.ds(g * GROUP, GROUP), :], stage_out.at[g])

    def give(g):
        for half in range(2):
            for p in range(positions):
                cells = halves[half, g * GROUP + HALO:(g + 1) * GROUP + HALO, p * half_of:(p + 1) * half_of, :]
                cells = cells.reshape(GROUP * half_of, lanes)[:, :wide]
                moved = jnp.dot(outward[...], cells, preferred_element_type=f32)[:, :width]
                stage[g, half * half_of:(half + 1) * half_of, p] = moved.reshape(half_of, GROUP, width).astype(bf16)
        store(g).start()

    done = [layer for layer in range(layers)]
    given = set()
    ahead = 2
    for q, (start, size) in enumerate(chunks):
        last = q == len(chunks) - 1
        if not last:
            sets = count // groups_of[q]
            early = max(0, sets - max(1, sets // 4))
            drained(q, 0, early)
            release(q + 1)
            drained(q, early, sets)
        gradient_rows(q)
        if q == 0:
            @pl.when(has_below)
            def _():
                merge_border(1)
        if last:
            @pl.when(has_above)
            def _():
                merge_border(0)
        end = start + size
        for layer in range(layers):
            high = end - 2 - layer if not last else rows + HALO - 2 - layer
            cover(layer, done[layer] + 1, high)
            done[layer] = max(done[layer], high)
            if last:
                cover(layer, layer + 1 - HALO, layer)
        for g in range(groups):
            if g not in given and (last or (g > 0 and (g + 1) * GROUP - 1 <= done[layers - 1])):
                given.add(g)
                give(g)

    for k in range(2):
        for p in range(positions):
            pltpu.sync_copy(summed.at[k, p, :, pl.ds(0, wide)], gradient_out.at[k, p])
    for g in range(groups):
        store(g).wait()

    @pl.when(has_above)
    def _():
        edge_left(1)

    @pl.when(has_below)
    def _():
        edge_left(0)

    @pl.loop(0, count)
    def _(c):
        all_of(send_out, c, out_sent)

    drained(len(chunks) - 1, 0, count // groups_of[-1])


def per_device(state, sens, kdata, mask, inject, kernels, biases, mixers):
    spaces, coils = lax.axis_size("space"), lax.axis_size("coil")
    channels, positions, rows, width = state.shape
    count, npar = sens.shape[1], sens.shape[4]
    held, npe = kdata.shape[3:]
    layers, _, outs, _ = kernels.shape
    sites = positions * rows
    unit = positions * outs
    wide = -(-width // 128) * 128
    lanes = -(-(width + 2 * HALO) // 128) * 128
    deep = rows + 2 * HALO + 8
    chunks = row_chunks(rows)
    vmem = pl.BlockSpec(memory_space=pltpu.VMEM)
    hbm = pl.BlockSpec(memory_space=pl.ANY)
    dma = pltpu.SemaphoreType.DMA
    groups = [packed(positions, size, count) for _, size in chunks]
    most = max(size for _, size in chunks)
    backs = [pltpu.VMEM((count // g, spaces, held, g * 2 * positions * size), bf16)
             for g, (_, size) in zip(groups, chunks)]
    shares = [pltpu.VMEM((coils, 2, positions * size, lanes), bf16) for _, size in chunks]
    message = pltpu.VMEM((count, spaces, held, 2 * sites), bf16)
    outer = 2 * positions * HALO
    new_state, gradient = pl.pallas_call(
        functools.partial(body, (spaces, coils, rows * spaces, npar, chunks)),
        out_shape=(
            jax.ShapeDtypeStruct(state.shape, bf16),
            jax.ShapeDtypeStruct((2, positions, rows, wide), f32),
        ),
        in_specs=[hbm] * 5 + [vmem] * 5,
        out_specs=(hbm, hbm),
        scratch_shapes=[
            pltpu.VMEM(sens.shape, f32),
            pltpu.VMEM(kdata.shape, f32),
            pltpu.VMEM(state.shape, bf16),
            pltpu.VMEM((2, npar, npar), bf16),
            pltpu.VMEM((2, npe, npe), bf16),
            pltpu.VMEM((coils, 2, positions, rows, width), bf16),
            pltpu.VMEM((2, sites, npar), f32),
            message, message, backs, backs,
            pltpu.VMEM((2, positions * most, npar), f32),
            shares, shares,
            pltpu.VMEM((2, coils, outer, lanes), bf16),
            pltpu.VMEM((2, coils, outer, lanes), bf16),
            pltpu.VMEM((2, deep, unit, lanes), bf16),
            pltpu.VMEM((2, 2, rows + 2 * HALO, unit, 128), bf16),
            pltpu.VMEM((2, 2, rows + 2 * HALO, unit, 128), bf16),
            pltpu.VMEM((layers, 3, BLOCK * unit, (BLOCK + 2) * unit), bf16),
            pltpu.VMEM((3, unit, (BLOCK + 2) * unit), f32),
            pltpu.VMEM((layers, BLOCK * unit, BLOCK * unit), bf16),
            pltpu.VMEM((layers, BLOCK * unit, 128), f32),
            pltpu.VMEM((2, 2, unit, 128), f32),
            pltpu.VMEM((GROUP * outs, GROUP * outs), bf16),
            pltpu.VMEM((GROUP * outs, GROUP * outs), bf16),
            pltpu.VMEM((rows // GROUP, channels, positions, GROUP, width), bf16),
            pltpu.VMEM((2, positions, rows, lanes), f32),
            dma((count,)), dma, dma, dma, dma, dma, dma((rows // GROUP,)), dma,
            dma((coils,)), dma((coils,)), dma((count,)), dma((count,)),
            [dma((count // g,)) for g in groups], [dma((count // g,)) for g in groups],
            dma((len(chunks), coils)), dma((len(chunks), coils)), dma((2, coils)), dma((2, coils)),
            dma((2,)), dma((2,)), dma((2,)), dma((2,)),
        ],
        compiler_params=pltpu.CompilerParams(
            collective_id=0, has_side_effects=True, vmem_limit_bytes=62 * 1024 * 1024),
    )(state, sens, kdata, dft_table(npar), dft_table(npe), mask, inject.T, kernels, biases, mixers)
    return new_state, gradient[..., :width]


def solution(mesh):
    return jax.shard_map(
        per_device,
        mesh=mesh,
        in_specs=(
            P(None, None, "space", "coil"),
            P(None, "coil", None, "space", None),
            P(None, "coil", None, "space", None),
            P("space", None),
            P(),
            P(),
            P(),
            P(),
        ),
        out_specs=(P(None, None, "space", "coil"), P(None, None, "space", "coil")),
        check_vma=False,
    )
```

```python
import functools
import math

import jax
import jax.numpy as jnp
import numpy as np
from jax import lax
from jax.experimental import pallas as pl
from jax.experimental.pallas import tpu as pltpu
from jax.sharding import PartitionSpec as P

HALO = 4
BLOCK = 6
GROUP = 16
TOGETHER = 5
f32, bf16 = jnp.float32, jnp.bfloat16


def dft_table(length):
    turns = np.arange(length)[:, None] * np.arange(length)[None, :] % length * (2.0 * math.pi / length)
    table = np.stack([np.cos(turns), np.sin(turns)]) / math.sqrt(length)
    return jnp.asarray(table.astype(np.float32).astype(bf16))


def row_chunks(rows):
    sizes = [rows // 2] if rows % (2 * GROUP) == 0 else []
    while sum(sizes) < rows:
        sizes.append(min(GROUP, rows - sum(sizes)))
    starts = [sum(sizes[:k]) for k in range(len(sizes))]
    return list(zip(starts, sizes))


def packed(positions, size, count):
    group = max(1, 128 // (2 * positions * size))
    while count % group:
        group -= 1
    return group


def column(row, length):
    ones = lax.broadcasted_iota(jnp.int32, (length, length), 0) == lax.broadcasted_iota(jnp.int32, (length, length), 1)
    return jnp.sum(jnp.where(ones, jnp.broadcast_to(row, (length, length)), 0.0), axis=1, keepdims=True)


def tap_choice(positions, ins, bands, po, c):
    lane = lax.broadcasted_iota(jnp.int32, (27, bands), 1)
    tap = lax.broadcasted_iota(jnp.int32, (27, bands), 0)
    offset = lane // ins % positions - po + 1
    row = lane // (ins * positions)
    wanted = (offset >= 0) & (offset < 3) & (row < 3) & (tap == 9 * offset + 3 * row + c)
    return jnp.where(wanted, 1.0, 0.0).astype(bf16)


def swapped(outer, inner):
    size = outer * inner
    to = lax.broadcasted_iota(jnp.int32, (size, size), 0)
    of = lax.broadcasted_iota(jnp.int32, (size, size), 1)
    same = (to // inner == of % outer) & (to % inner == of // outer)
    return jnp.where(same, 1.0, 0.0).astype(bf16)


def body(dims, state_hbm, sens_hbm, kdata_hbm, par_hbm, pe_hbm, mask_ref, inject_ref, kernel_ref, bias_ref, mixer_ref,
         state_out, gradient_out,
         sens_ref, kdata_ref, state_ref, par_ref, pe_ref,
         seen, whole, send_out, got_out, send_back, got_back, total, part, parts, edge, edges,
         halves, strips, borders, weight, strip, mix, bias, spread, inward, summed,
         sens_in, kdata_in, state_in, par_in, pe_in, est_in, stage_out, summed_out,
         seen_sent, seen_got, out_sent, out_got, back_sent, back_got, part_sent, part_got, edge_sent, edge_got,
         row_sent, row_got, col_sent, col_got):
    spaces, coils, total_rows, total_cols, chunks = dims
    mesh_id = pl.DeviceIdType.MESH
    space = lax.axis_index("space")
    coil = lax.axis_index("coil")
    channels, positions, rows, width = state_ref.shape
    half_of = channels // 2
    unit = positions * half_of
    layers = kernel_ref.shape[0]
    count, npar = sens_ref.shape[1], sens_ref.shape[4]
    held, npe = kdata_ref.shape[3:]
    lanes = halves.shape[3]
    deep = halves.shape[1]
    sites = positions * rows
    lines = positions * held
    has_above, has_below = space > 0, space < spaces - 1
    has_left, has_right = coil > 0, coil < coils - 1

    def turn(value, step, size):
        return lax.rem(value + step + size, size)

    fetch_par = pltpu.make_async_copy(par_hbm, par_ref, par_in)
    fetch_pe = pltpu.make_async_copy(pe_hbm, pe_ref, pe_in)
    fetch_kdata = pltpu.make_async_copy(kdata_hbm, kdata_ref, kdata_in)

    def fetch_state(g):
        at = pl.ds(g * GROUP, GROUP)
        return pltpu.make_async_copy(state_hbm.at[:, :, at, :], state_ref.at[:, :, at, :], state_in.at[g])

    fetch_estimate = pltpu.make_async_copy(state_hbm.at[0:2], seen.at[coil], est_in)

    def fetch_sens(c):
        return pltpu.make_async_copy(sens_hbm.at[:, c], sens_ref.at[:, c], sens_in.at[c])

    groups = rows // GROUP
    edge_groups = sorted({0, groups - 1})
    lead = min(2, count)
    fetch_estimate.start()
    for g in edge_groups:
        fetch_state(g).start()
    fetch_par.start()
    for c in range(lead):
        fetch_sens(c).start()

    inward[...] = swapped(GROUP, half_of)
    barrier = pltpu.get_barrier_semaphore()

    @pl.loop(1, spaces)
    def _(offset):
        pl.semaphore_signal(barrier, inc=1, device_id={"space": lax.rem(space + offset, spaces)}, device_id_type=mesh_id)

    for offset in range(1, coils):
        other = lax.rem(coil + offset, coils)
        pl.semaphore_signal(barrier, inc=1, device_id={"coil": other}, device_id_type=mesh_id)
        for step in (1, -1):
            pl.semaphore_signal(barrier, inc=1, device_id={"space": turn(space, step, spaces), "coil": other},
                                device_id_type=mesh_id)
    pl.semaphore_wait(barrier, spaces - 1 + 3 * (coils - 1))

    def to_coil(source, target, offset, sent, got):
        return pltpu.make_async_remote_copy(
            src_ref=source, dst_ref=target, send_sem=sent.at[offset], recv_sem=got.at[offset],
            device_id={"coil": lax.rem(coil + offset, coils)}, device_id_type=mesh_id)

    def to_space(buffer, target, c, offset, sent, got):
        other = lax.rem(space + offset, spaces)
        return pltpu.make_async_remote_copy(
            src_ref=buffer.at[c, other], dst_ref=target.at[c, space], send_sem=sent.at[c], recv_sem=got.at[c],
            device_id={"space": other}, device_id_type=mesh_id)

    def send_all(buffer, target, c, sent, got):
        @pl.loop(1, spaces)
        def _(offset):
            to_space(buffer, target, c, offset, sent, got).start()

    def all_of(buffer, c, sem):
        span = buffer.at[c, pl.ds(0, spaces - 1)]
        pltpu.make_async_copy(span, span, sem.at[c]).wait()

    for offset in range(1, coils):
        to_coil(state_hbm.at[0:2], seen.at[coil], offset, seen_sent, seen_got).start()

    def clear(row, many):
        for half in range(2):
            halves[half, pl.ds(row, many)] = jnp.zeros((many, unit, lanes), bf16)

    def row_major(g):
        at = pl.ds(pl.multiple_of(g * GROUP, GROUP), GROUP)
        into = pl.ds(g * GROUP + HALO, GROUP)
        for half in range(2):
            for p in range(positions):
                cells = state_ref[half * half_of:(half + 1) * half_of, p, at, :].reshape(half_of * GROUP, width)
                moved = jnp.dot(inward[...], cells, preferred_element_type=f32)
                moved = moved.reshape(GROUP, half_of, width).astype(bf16)
                if lanes > width:
                    moved = jnp.concatenate([moved, jnp.zeros((GROUP, half_of, lanes - width), bf16)], axis=-1)
                halves[half, into, p * half_of:(p + 1) * half_of, :] = moved

    def upright(way):
        source, target = (rows, HALO)[way], (0, HALO + rows)[way]
        return pltpu.make_async_remote_copy(
            src_ref=halves.at[:, pl.ds(source, HALO), :, pl.ds(0, wide)],
            dst_ref=halves.at[:, pl.ds(target, HALO), :, pl.ds(0, wide)],
            send_sem=row_sent.at[way], recv_sem=row_got.at[way],
            device_id={"space": turn(space, (1, -1)[way], spaces)}, device_id_type=mesh_id)

    wide = -(-width // 128) * 128
    for g in edge_groups:
        fetch_state(g).wait()

    @pl.when(space == 0)
    def _():
        clear(0, HALO)

    @pl.when(space == spaces - 1)
    def _():
        clear(HALO + rows, HALO)

    if wide < lanes:
        for first in (0, HALO + rows):
            halves[:, pl.ds(first, HALO), :, wide:lanes] = jnp.zeros((2, HALO, unit, lanes - wide), bf16)
    row_major(0)

    @pl.when(has_above)
    def _():
        upright(1).start()

    if groups > 1:
        row_major(groups - 1)

    @pl.when(has_below)
    def _():
        upright(0).start()

    fetch_estimate.wait()
    fetch_par.wait()
    for offset in range(1, coils):
        to_coil(state_hbm.at[0:2], seen.at[coil], offset, seen_sent, seen_got).wait()
    for k in range(2):
        whole[k] = jnp.concatenate([seen[j, k].astype(f32).reshape(sites, width) for j in range(coils)], axis=-1)

    @pl.loop(lead, count)
    def _(c):
        fetch_sens(c).start()

    for g in range(1, groups - 1):
        fetch_state(g).start()

    def coil_image(c):
        fetch_sens(c).wait()
        profile_real = sens_ref[0, c].reshape(sites, npar)
        profile_imag = sens_ref[1, c].reshape(sites, npar)
        real = profile_real * whole[0] - profile_imag * whole[1]
        imag = profile_real * whole[1] + profile_imag * whole[0]
        plain = jnp.concatenate([real, imag], axis=0).astype(bf16)
        turned = jnp.concatenate([imag, -real], axis=0).astype(bf16)
        along = (((1,), (1,)), ((), ()))
        spectrum = lax.dot_general(par_ref[0], plain, along, preferred_element_type=f32)
        spectrum += lax.dot_general(par_ref[1], turned, along, preferred_element_type=f32)
        send_out[c] = spectrum.reshape(spaces, held, 2 * sites).astype(bf16)
        got_out[c, space] = send_out[c, space]

    window = min(3, count)

    @pl.loop(0, window)
    def _(c):
        coil_image(c)
        send_all(send_out, got_out, c, out_sent, out_got)

    fetch_pe.start()
    fetch_kdata.start()

    if groups > 2:
        for g in range(1, groups - 1):
            fetch_state(g).wait()

        @pl.loop(1, groups - 1)
        def _(g):
            row_major(g)

    clear(rows + 2 * HALO, deep - rows - 2 * HALO)

    bands = unit * (BLOCK + 2)
    pixel = lax.broadcasted_iota(jnp.int32, (half_of * half_of, bands), 0)
    same_in = pixel % half_of == lax.broadcasted_iota(jnp.int32, (half_of * half_of, bands), 1) % half_of
    outs_of = lax.broadcasted_iota(jnp.int32, (half_of, half_of * half_of), 1) // half_of
    outs_of = jnp.where(outs_of == lax.broadcasted_iota(jnp.int32, outs_of.shape, 0), 1.0, 0.0).astype(bf16)

    @pl.loop(0, layers)
    def _(k):
        taps = kernel_ref[k].reshape(half_of * half_of, 27)
        for c in range(3):
            for po in range(positions):
                chosen = jnp.dot(taps, tap_choice(positions, half_of, bands, po, c), preferred_element_type=f32)
                chosen = jnp.where(same_in, chosen, 0.0).astype(bf16)
                strip[c, po * half_of:(po + 1) * half_of, :] = jnp.dot(outs_of, chosen, preferred_element_type=f32)
        for c in range(3):
            for x in range(BLOCK):
                line = pltpu.roll(strip[c], unit * x, 1) if x else strip[c]
                weight[k, c * BLOCK * unit + unit * x:c * BLOCK * unit + unit * (x + 1), :] = line[:, :bands].astype(bf16)
        own = mixer_ref[k].astype(f32)
        times = positions * BLOCK
        for x in range(times):
            parts_of = [jnp.zeros((half_of, half_of * x), f32)] if x else []
            parts_of.append(own)
            if x < times - 1:
                parts_of.append(jnp.zeros((half_of, half_of * (times - 1 - x)), f32))
            mix[k, half_of * x:half_of * (x + 1), :] = jnp.concatenate(parts_of, axis=-1).astype(bf16)
        offsets = column(bias_ref[pl.ds(k, 1), :], half_of)
        bias[k] = jnp.concatenate([jnp.broadcast_to(offsets, (half_of, 128))] * times, axis=0)

    for half in range(2):
        for g in range(2):
            gains = column(inject_ref[g:g + 1, half * half_of:(half + 1) * half_of], half_of)
            spread[half, g] = jnp.concatenate([jnp.broadcast_to(gains, (half_of, 128))] * positions, axis=0)

    @pl.when(has_below)
    def _():
        upright(0).wait_send()
        upright(1).wait_recv()

    @pl.when(has_above)
    def _():
        upright(1).wait_send()
        upright(0).wait_recv()

    lane = lax.broadcasted_iota(jnp.int32, (1, lanes), 1)

    @pl.loop(0, rows + 2 * HALO)
    def _(row):
        for half in range(2):
            line = jnp.where(lane < width, halves[half, row].astype(f32), 0.0)
            strips[0, half, row] = pltpu.roll(line, lanes - width, 1)[:, lanes - 128:].astype(bf16)
            strips[1, half, row] = pltpu.roll(line, width, 1)[:, lanes - 128:].astype(bf16)

    def sideways(way):
        return pltpu.make_async_remote_copy(
            src_ref=strips.at[way], dst_ref=borders.at[way], send_sem=col_sent.at[way], recv_sem=col_got.at[way],
            device_id={"coil": turn(coil, (1, -1)[way], coils)}, device_id_type=mesh_id)

    @pl.when(has_right)
    def _():
        sideways(0).start()

    @pl.when(has_left)
    def _():
        sideways(1).start()

    final = lax.broadcasted_iota(jnp.int32, (1, 128), 1)

    def blend(way, inside):
        @pl.loop(0, rows + 2 * HALO)
        def _(row):
            for half in range(2):
                own = halves[half, row, :, lanes - 128:].astype(f32)
                new = borders[way, half, row].astype(f32)
                halves[half, row, :, lanes - 128:] = jnp.where(inside, new, own).astype(bf16)

    @pl.when(has_left)
    def _():
        sideways(0).wait_recv()
        blend(0, final >= 128 - HALO)

    @pl.when(has_right)
    def _():
        sideways(1).wait_recv()
        first = width % 128
        blend(1, (final >= first) & (final < first + HALO))

    @pl.when(has_right)
    def _():
        sideways(0).wait_send()

    @pl.when(has_left)
    def _():
        sideways(1).wait_send()

    @pl.loop(window, count)
    def _(c):
        coil_image(c)
        all_of(send_out, c - window, out_sent)
        send_all(send_out, got_out, c, out_sent, out_got)

    fetch_pe.wait()
    fetch_kdata.wait()
    pair = max(packed(positions, size, count) for _, size in chunks)
    groups_of = [packed(positions, size, count) for _, size in chunks]

    @pl.loop(0, count // pair)
    def _(couple):
        backs = []
        for j in range(pair):
            c = couple * pair + j
            all_of(got_out, c, out_got)
            blocks = [got_out[c, s].astype(f32) for s in range(spaces)]
            grid = [
                jnp.concatenate([block[:, k * rows:(k + 1) * rows] for block in blocks], axis=-1)
                for k in range(2 * positions)
            ]
            real = jnp.concatenate(grid[:positions], axis=0)
            imag = jnp.concatenate(grid[positions:], axis=0)
            plain = jnp.concatenate([real, imag], axis=0).astype(bf16)
            turned = jnp.concatenate([imag, -real], axis=0).astype(bf16)
            full = jnp.dot(plain, pe_ref[0], preferred_element_type=f32)
            full += jnp.dot(turned, pe_ref[1], preferred_element_type=f32)
            sampled = jnp.concatenate([mask_ref[...].astype(f32)] * positions, axis=0)
            real = sampled * (full[:lines] - kdata_ref[0, c].reshape(lines, npe))
            imag = sampled * (full[lines:] - kdata_ref[1, c].reshape(lines, npe))
            plain = jnp.concatenate([real, imag], axis=0).astype(bf16)
            turned = jnp.concatenate([-imag, real], axis=0).astype(bf16)
            back = jnp.dot(plain, pe_ref[0], preferred_element_type=f32)
            back += jnp.dot(turned, pe_ref[1], preferred_element_type=f32)
            backs.append(back)
            for q, (start, size) in enumerate(chunks):
                many = groups_of[q]
                if (j + 1) % many:
                    continue
                c_group = couple * (pair // many) + j // many
                for s in range(spaces):
                    send_back[q][c_group, s] = jnp.concatenate(
                        [backs[i][k * held:(k + 1) * held, s * rows + start:s * rows + start + size]
                         for i in range(j + 1 - many, j + 1) for k in range(2 * positions)], axis=-1
                    ).astype(bf16)
                got_back[q][c_group, space] = send_back[q][c_group, space]
                if q == 0:
                    send_all(send_back[q], got_back[q], c_group, back_sent[q], back_got[q])

    def release(q):
        sets = count // groups_of[q]

        @pl.loop(0, sets)
        def _(g):
            send_all(send_back[q], got_back[q], g, back_sent[q], back_got[q])

    def drained(q, low, high):
        @pl.loop(low, high)
        def _(g):
            all_of(send_back[q], g, back_sent[q])

    column_at = jnp.where(lane >= lanes - HALO, lane - lanes, lane) + coil * width
    good = (column_at >= 0) & (column_at < total_cols) & ((lane < width + HALO) | (lane >= lanes - HALO))
    column_ok = jnp.where(good, 1.0, 0.0)
    end_ok = column_ok[:, lanes - 128:]

    def extended(value, j):
        after = min(npar, (j + 1) * width + HALO) - j * width
        before = HALO if j else 0
        room = lanes - width
        if j == 0 and lanes <= npar:
            return value[:, :lanes]
        if j == coils - 1 and j * width >= room:
            return jnp.concatenate([value[:, j * width:], value[:, j * width - room:j * width]], axis=-1)
        pieces = [value[:, j * width:j * width + after], jnp.zeros((value.shape[0], lanes - after - before), f32)]
        if before:
            pieces.append(value[:, j * width - before:j * width])
        return jnp.concatenate(pieces, axis=-1)

    def edgeways(way, j):
        return pltpu.make_async_remote_copy(
            src_ref=edge.at[way, j], dst_ref=edges.at[way, coil],
            send_sem=edge_sent.at[way, j], recv_sem=edge_got.at[way, coil],
            device_id={"space": turn(space, (1, -1)[way], spaces), "coil": j}, device_id_type=mesh_id)

    def edge_landed(way):
        for j in range(coils):
            pltpu.make_async_copy(edges.at[way, j], edges.at[way, j], edge_got.at[way, j]).wait()

    def edge_left(way):
        for j in range(coils):
            pltpu.make_async_copy(edge.at[way, j], edge.at[way, j], edge_sent.at[way, j]).wait()

    def limit(value):
        if lanes > 128:
            return jnp.concatenate([value[:, :lanes - 128], value[:, lanes - 128:] * end_ok], axis=-1)
        return value * end_ok

    def merge(row, lines_of):
        spreads = [
            jnp.concatenate([jnp.broadcast_to(lines_of[g][p], (half_of, lanes)) for p in range(positions)], axis=0)
            for g in range(2)
        ]
        for half in range(2):
            gains = [jnp.concatenate([spread[half, g]] * (lanes // 128), axis=-1) for g in range(2)]
            added = gains[0] * spreads[0] + gains[1] * spreads[1]
            halves[half, row] = (halves[half, row].astype(f32) + added).astype(bf16)

    def send_rows(q):
        start, size = chunks[q]
        many = groups_of[q]
        sets = count // many
        spots = positions * size
        at_once = max(1, 256 // (many * 2 * spots))
        while sets % at_once:
            at_once -= 1
        total[:, :spots] = jnp.zeros((2, spots, npar), f32)

        @pl.loop(0, sets // at_once)
        def _(step):
            plains, turneds = [], []
            for i in range(at_once):
                g = step * at_once + i
                all_of(got_back[q], g, back_got[q])
                value = got_back[q][g].astype(f32).reshape(npar, many * 2 * spots)
                plains.append(value)
                for j in range(many):
                    base = j * 2 * spots
                    turneds += [-value[:, base + spots:base + 2 * spots], value[:, base:base + spots]]
            plain = jnp.concatenate(plains, axis=-1).astype(bf16)
            turned = jnp.concatenate(turneds, axis=-1).astype(bf16)
            along = (((0,), (0,)), ((), ()))
            image = lax.dot_general(plain, par_ref[0], along, preferred_element_type=f32)
            image += lax.dot_general(turned, par_ref[1], along, preferred_element_type=f32)
            for i in range(at_once * many):
                c = step * (at_once * many) + i
                base = i * 2 * spots
                real, imag = image[base:base + spots], image[base + spots:base + 2 * spots]
                profile_real = sens_ref[0, c, :, start:start + size, :].reshape(spots, npar)
                profile_imag = sens_ref[1, c, :, start:start + size, :].reshape(spots, npar)
                total[0, :spots] += profile_real * real + profile_imag * imag
                total[1, :spots] += profile_real * imag - profile_imag * real

        for j in range(coils):
            for k in range(2):
                part[q][j, k] = extended(total[k, :spots], j).astype(bf16)
        for offset in range(1, coils):
            to_coil(part[q].at[lax.rem(coil + offset, coils)], parts[q].at[coil], offset, part_sent.at[q], part_got.at[q]).start()
        parts[q][coil] = part[q][coil]

        def put_edge(way, low):
            for j in range(coils):
                edge[way, j] = jnp.concatenate(
                    [extended(total[k, p * size + low:p * size + low + HALO], j) for k in range(2) for p in range(positions)],
                    axis=0).astype(bf16)

            @pl.when((has_below, has_above)[way])
            def _():
                for j in range(coils):
                    edgeways(way, j).start()

        if q == 0:
            put_edge(1, 0)
        if q == len(chunks) - 1:
            put_edge(0, size - HALO)

    def land_rows(q):
        start, size = chunks[q]
        for offset in range(1, coils):
            to_coil(part[q].at[lax.rem(coil + offset, coils)], parts[q].at[coil], offset, part_sent.at[q], part_got.at[q]).wait()
        for k in range(2):
            value = parts[q][0, k].astype(f32)
            for j in range(1, coils):
                value += parts[q][j, k].astype(f32)
            value = limit(value)
            for p in range(positions):
                summed[k, p, start:start + size, :] = value[p * size:(p + 1) * size]

        @pl.loop(start, start + size)
        def _(row):
            merge(row + HALO, [[summed[g, p, pl.ds(row, 1), :] for p in range(positions)] for g in range(2)])

    def merge_border(way):
        first = (0, HALO + rows)[way]
        edge_landed(way)
        value = edges[way, 0].astype(f32)
        for j in range(1, coils):
            value += edges[way, j].astype(f32)
        value = limit(value)
        for r in range(HALO):
            merge(first + r, [
                [value[(g * positions + p) * HALO + r:(g * positions + p) * HALO + r + 1] for p in range(positions)]
                for g in range(2)
            ])

    def cell_rows(layer, blocks):
        source, target = layer % 2, 1 - layer % 2
        high = BLOCK * unit
        news = []
        for row, keep, inner in blocks:
            cells = halves[source, pl.ds(row - 1, BLOCK + 2)].reshape((BLOCK + 2) * unit, lanes)
            taps = jnp.dot(weight[layer], cells, preferred_element_type=f32)
            raw = pltpu.roll(taps[:high], 1, 1) + taps[high:2 * high] + pltpu.roll(taps[2 * high:], lanes - 1, 1)
            hidden = jnp.maximum(raw + jnp.concatenate([bias[layer]] * (lanes // 128), axis=-1), 0.0)
            hidden = limit(hidden)
            if not inner:
                step = lax.broadcasted_iota(jnp.int32, (high, 1), 0) // unit
                at = step + (row - HALO + space * rows)
                hidden = jnp.where((at >= 0) & (at < total_rows), hidden, 0.0)
            update = jnp.dot(mix[layer], hidden.astype(bf16), preferred_element_type=f32)
            if keep < BLOCK:
                update = update[:keep * unit]
            old = halves[target, pl.ds(row, keep)].astype(f32)
            news.append((old + update.reshape(keep, unit, lanes)).astype(bf16))
        for (row, keep, _), new in zip(blocks, news):
            halves[target, pl.ds(row, keep)] = new

    def blocks_of(low, high):
        found = []
        row = low
        while row <= high:
            keep = min(BLOCK, high - row + 1)
            found.append((row + HALO, keep, row >= 0 and row + keep <= rows))
            row += keep
        return found

    def cover(layer, low, high, more=()):
        blocks = blocks_of(low, high)
        blocks += list(more)
        for k in range(0, len(blocks), TOGETHER):
            cell_rows(layer, blocks[k:k + TOGETHER])

    def give(half):
        return pltpu.make_async_copy(
            halves.at[half, pl.ds(HALO, rows), :, pl.ds(0, wide)], state_out.at[half], stage_out.at[half])

    give_gradient = pltpu.make_async_copy(summed.at[:, :, :, pl.ds(0, wide)], gradient_out, summed_out)

    def follow(q):
        sets = count // groups_of[q]
        early = max(0, sets - max(1, sets // 4))
        drained(q, 0, early)
        release(q + 1)
        drained(q, early, sets)

    done = [layer for layer in range(layers)]
    def couplings(q, which):
        last = q == len(chunks) - 1
        end = sum(chunks[q])
        for layer in which:
            high = end - 2 - layer if not last else rows + HALO - 2 - layer
            cover(layer, done[layer] + 1, high, blocks_of(layer + 1 - HALO, layer) if last else ())
            done[layer] = max(done[layer], high)
            if last and layer >= layers - 2:
                give(1 - layer % 2).start()

    if len(chunks) > 1:
        follow(0)
    send_rows(0)
    land_rows(0)

    @pl.when(has_below)
    def _():
        merge_border(1)

    for q in range(len(chunks) - 1):
        couplings(q, range(layers // 2))
        if q + 2 < len(chunks):
            follow(q + 1)
        send_rows(q + 1)
        couplings(q, range(layers // 2, layers))
        land_rows(q + 1)

    give_gradient.start()

    @pl.when(has_above)
    def _():
        merge_border(0)

    couplings(len(chunks) - 1, range(layers))
    give_gradient.wait()
    for half in range(2):
        give(half).wait()

    @pl.when(has_above)
    def _():
        edge_left(1)

    @pl.when(has_below)
    def _():
        edge_left(0)

    @pl.loop(count - window, count)
    def _(c):
        all_of(send_out, c, out_sent)

    drained(len(chunks) - 1, 0, count // groups_of[-1])


def finish(half_of, cells_hbm, gradient_hbm, state_out, gradient_out,
           cells_ref, stage, summed, trimmed, outward, cells_in, stage_out, summed_in, summed_out):
    width = state_out.shape[3]
    _, rows, _, wide = cells_hbm.shape
    groups = rows // GROUP

    def fetch(g):
        at = pl.ds(g * GROUP, GROUP)
        return pltpu.make_async_copy(cells_hbm.at[:, at], cells_ref.at[:, at], cells_in.at[g])

    def store(g):
        at = pl.ds(g * GROUP, GROUP)
        return pltpu.make_async_copy(stage.at[:, :, at, :], state_out.at[:, :, at, :], stage_out.at[g])

    fetch_gradient = pltpu.make_async_copy(gradient_hbm, summed, summed_in)
    store_gradient = pltpu.make_async_copy(summed if wide == width else trimmed, gradient_out, summed_out)
    for g in range(groups):
        fetch(g).start()
    fetch_gradient.start()
    outward[...] = swapped(half_of, GROUP)
    for g in range(groups):
        fetch(g).wait()
        for half in range(2):
            for p in range(state_out.shape[1]):
                cells = cells_ref[half, g * GROUP:(g + 1) * GROUP, p * half_of:(p + 1) * half_of, :]
                moved = jnp.dot(outward[...], cells.reshape(GROUP * half_of, wide), preferred_element_type=f32)
                moved = moved[:, :width].reshape(half_of, GROUP, width).astype(bf16)
                stage[half * half_of:(half + 1) * half_of, p, g * GROUP:(g + 1) * GROUP, :] = moved
        store(g).start()
    fetch_gradient.wait()
    if wide != width:
        trimmed[...] = summed[:, :, :, :width]
    store_gradient.start()
    for g in range(groups):
        store(g).wait()
    store_gradient.wait()


def per_device(state, sens, kdata, mask, inject, kernels, biases, mixers):
    spaces, coils = lax.axis_size("space"), lax.axis_size("coil")
    channels, positions, rows, width = state.shape
    count, npar = sens.shape[1], sens.shape[4]
    held, npe = kdata.shape[3:]
    layers, _, outs, _ = kernels.shape
    sites = positions * rows
    unit = positions * outs
    wide = -(-width // 128) * 128
    lanes = -(-(width + 2 * HALO) // 128) * 128
    deep = rows + 2 * HALO + 8
    chunks = row_chunks(rows)
    vmem = pl.BlockSpec(memory_space=pltpu.VMEM)
    hbm = pl.BlockSpec(memory_space=pl.ANY)
    dma = pltpu.SemaphoreType.DMA
    groups = [packed(positions, size, count) for _, size in chunks]
    most = max(size for _, size in chunks)
    backs = [pltpu.VMEM((count // g, spaces, held, g * 2 * positions * size), bf16)
             for g, (_, size) in zip(groups, chunks)]
    shares = [pltpu.VMEM((coils, 2, positions * size, lanes), bf16) for _, size in chunks]
    message = pltpu.VMEM((count, spaces, held, 2 * sites), bf16)
    outer = 2 * positions * HALO
    cells, gradient = pl.pallas_call(
        functools.partial(body, (spaces, coils, rows * spaces, npar, chunks)),
        out_shape=(
            jax.ShapeDtypeStruct((2, rows, unit, wide), bf16),
            jax.ShapeDtypeStruct((2, positions, rows, wide), f32),
        ),
        in_specs=[hbm] * 5 + [vmem] * 5,
        out_specs=(hbm, hbm),
        scratch_shapes=[
            pltpu.VMEM(sens.shape, f32),
            pltpu.VMEM(kdata.shape, f32),
            pltpu.VMEM(state.shape, bf16),
            pltpu.VMEM((2, npar, npar), bf16),
            pltpu.VMEM((2, npe, npe), bf16),
            pltpu.VMEM((coils, 2, positions, rows, width), bf16),
            pltpu.VMEM((2, sites, npar), f32),
            message, message, backs, backs,
            pltpu.VMEM((2, positions * most, npar), f32),
            shares, shares,
            pltpu.VMEM((2, coils, outer, lanes), bf16),
            pltpu.VMEM((2, coils, outer, lanes), bf16),
            pltpu.VMEM((2, deep, unit, lanes), bf16),
            pltpu.VMEM((2, 2, rows + 2 * HALO, unit, 128), bf16),
            pltpu.VMEM((2, 2, rows + 2 * HALO, unit, 128), bf16),
            pltpu.VMEM((layers, 3 * BLOCK * unit, (BLOCK + 2) * unit), bf16),
            pltpu.VMEM((3, unit, (BLOCK + 2) * unit), f32),
            pltpu.VMEM((layers, BLOCK * unit, BLOCK * unit), bf16),
            pltpu.VMEM((layers, BLOCK * unit, 128), f32),
            pltpu.VMEM((2, 2, unit, 128), f32),
            pltpu.VMEM((GROUP * outs, GROUP * outs), bf16),
            pltpu.VMEM((2, positions, rows, lanes), f32),
            dma((count,)), dma, dma((rows // GROUP,)), dma, dma, dma, dma((2,)), dma,
            dma((coils,)), dma((coils,)), dma((count,)), dma((count,)),
            [dma((count // g,)) for g in groups], [dma((count // g,)) for g in groups],
            dma((len(chunks), coils)), dma((len(chunks), coils)), dma((2, coils)), dma((2, coils)),
            dma((2,)), dma((2,)), dma((2,)), dma((2,)),
        ],
        compiler_params=pltpu.CompilerParams(
            collective_id=0, has_side_effects=True, vmem_limit_bytes=62 * 1024 * 1024),
    )(state, sens, kdata, dft_table(npar), dft_table(npe), mask, inject.T,
      jnp.transpose(kernels, (0, 2, 3, 1)), biases, mixers)
    return pl.pallas_call(
        functools.partial(finish, outs),
        out_shape=(
            jax.ShapeDtypeStruct(state.shape, bf16),
            jax.ShapeDtypeStruct((2, positions, rows, width), f32),
        ),
        in_specs=[hbm] * 2,
        out_specs=(hbm, hbm),
        scratch_shapes=[
            pltpu.VMEM((2, rows, unit, wide), bf16),
            pltpu.VMEM(state.shape, bf16),
            pltpu.VMEM((2, positions, rows, wide), f32),
            pltpu.VMEM((2, positions, rows, width), f32),
            pltpu.VMEM((GROUP * outs, GROUP * outs), bf16),
            dma((rows // GROUP,)), dma((rows // GROUP,)), dma, dma,
        ],
        compiler_params=pltpu.CompilerParams(vmem_limit_bytes=60 * 1024 * 1024),
    )(cells, gradient)


def solution(mesh):
    return jax.shard_map(
        per_device,
        mesh=mesh,
        in_specs=(
            P(None, None, "space", "coil"),
            P(None, "coil", None, "space", None),
            P(None, "coil", None, "space", None),
            P("space", None),
            P(),
            P(),
            P(),
            P(),
        ),
        out_specs=(P(None, None, "space", "coil"), P(None, None, "space", "coil")),
        check_vma=False,
    )
```

```python
import functools
import math

import jax
import jax.numpy as jnp
import numpy as np
from jax import lax
from jax.experimental import pallas as pl
from jax.experimental.pallas import tpu as pltpu
from jax.sharding import PartitionSpec as P

HALO = 4
BLOCK = 6
GROUP = 16
TOGETHER = 5
f32, bf16 = jnp.float32, jnp.bfloat16


def dft_table(length):
    turns = np.arange(length)[:, None] * np.arange(length)[None, :] % length * (2.0 * math.pi / length)
    table = np.stack([np.cos(turns), np.sin(turns)]) / math.sqrt(length)
    return jnp.asarray(table.astype(np.float32).astype(bf16))


def row_chunks(rows):
    sizes = [rows // 2] if rows % (2 * GROUP) == 0 else []
    while sum(sizes) < rows:
        sizes.append(min(GROUP, rows - sum(sizes)))
    starts = [sum(sizes[:k]) for k in range(len(sizes))]
    return list(zip(starts, sizes))


def packed(positions, size, count):
    group = max(1, 128 // (2 * positions * size))
    while count % group:
        group -= 1
    return group


def column(row, length):
    ones = lax.broadcasted_iota(jnp.int32, (length, length), 0) == lax.broadcasted_iota(jnp.int32, (length, length), 1)
    return jnp.sum(jnp.where(ones, jnp.broadcast_to(row, (length, length)), 0.0), axis=1, keepdims=True)


def tap_choice(positions, ins, bands, po, c):
    lane = lax.broadcasted_iota(jnp.int32, (27, bands), 1)
    tap = lax.broadcasted_iota(jnp.int32, (27, bands), 0)
    offset = lane // ins % positions - po + 1
    row = lane // (ins * positions)
    wanted = (offset >= 0) & (offset < 3) & (row < 3) & (tap == 9 * offset + 3 * row + c)
    return jnp.where(wanted, 1.0, 0.0).astype(bf16)


def swapped(outer, inner):
    size = outer * inner
    to = lax.broadcasted_iota(jnp.int32, (size, size), 0)
    of = lax.broadcasted_iota(jnp.int32, (size, size), 1)
    same = (to // inner == of % outer) & (to % inner == of // outer)
    return jnp.where(same, 1.0, 0.0).astype(bf16)


def body(dims, state_hbm, sens_hbm, kdata_hbm, par_hbm, pe_hbm, mask_ref, inject_ref, kernel_ref, bias_ref, mixer_ref,
         state_out, gradient_out,
         sens_ref, kdata_ref, state_ref, par_ref, pe_ref,
         seen, whole, send_out, got_out, send_back, got_back, total, part, parts, edge, edges,
         halves, strips, borders, weight, strip, mix, bias, spread, inward, summed,
         sens_in, kdata_in, state_in, par_in, pe_in, est_in, stage_out, summed_out,
         seen_sent, seen_got, out_sent, out_got, back_sent, back_got, part_sent, part_got, edge_sent, edge_got,
         row_sent, row_got, col_sent, col_got):
    spaces, coils, total_rows, total_cols, chunks = dims
    mesh_id = pl.DeviceIdType.MESH
    space = lax.axis_index("space")
    coil = lax.axis_index("coil")
    channels, positions, rows, width = state_ref.shape
    half_of = channels // 2
    unit = positions * half_of
    layers = kernel_ref.shape[0]
    count, npar = sens_ref.shape[1], sens_ref.shape[4]
    held, npe = kdata_ref.shape[3:]
    lanes = halves.shape[3]
    deep = halves.shape[1]
    sites = positions * rows
    lines = positions * held
    has_above, has_below = space > 0, space < spaces - 1
    has_left, has_right = coil > 0, coil < coils - 1

    def turn(value, step, size):
        return lax.rem(value + step + size, size)

    fetch_par = pltpu.make_async_copy(par_hbm, par_ref, par_in)
    fetch_pe = pltpu.make_async_copy(pe_hbm, pe_ref, pe_in)
    fetch_kdata = pltpu.make_async_copy(kdata_hbm, kdata_ref, kdata_in)

    def fetch_state(g):
        at = pl.ds(g * GROUP, GROUP)
        return pltpu.make_async_copy(state_hbm.at[:, :, at, :], state_ref.at[:, :, at, :], state_in.at[g])

    fetch_estimate = pltpu.make_async_copy(state_hbm.at[0:2], seen.at[coil], est_in)

    def fetch_sens(c):
        return pltpu.make_async_copy(sens_hbm.at[:, c], sens_ref.at[:, c], sens_in.at[c])

    groups = rows // GROUP
    edge_groups = sorted({0, groups - 1})
    lead = min(2, count)
    fetch_estimate.start()
    for g in edge_groups:
        fetch_state(g).start()
    fetch_par.start()
    for c in range(lead):
        fetch_sens(c).start()

    inward[...] = swapped(GROUP, half_of)
    barrier = pltpu.get_barrier_semaphore()

    @pl.loop(1, spaces)
    def _(offset):
        pl.semaphore_signal(barrier, inc=1, device_id={"space": lax.rem(space + offset, spaces)}, device_id_type=mesh_id)

    for offset in range(1, coils):
        other = lax.rem(coil + offset, coils)
        pl.semaphore_signal(barrier, inc=1, device_id={"coil": other}, device_id_type=mesh_id)
        for step in (1, -1):
            pl.semaphore_signal(barrier, inc=1, device_id={"space": turn(space, step, spaces), "coil": other},
                                device_id_type=mesh_id)
    pl.semaphore_wait(barrier, spaces - 1 + 3 * (coils - 1))

    def to_coil(source, target, offset, sent, got):
        return pltpu.make_async_remote_copy(
            src_ref=source, dst_ref=target, send_sem=sent.at[offset], recv_sem=got.at[offset],
            device_id={"coil": lax.rem(coil + offset, coils)}, device_id_type=mesh_id)

    def to_space(buffer, target, c, offset, sent, got):
        other = lax.rem(space + offset, spaces)
        return pltpu.make_async_remote_copy(
            src_ref=buffer.at[c, other], dst_ref=target.at[c, space], send_sem=sent.at[c], recv_sem=got.at[c],
            device_id={"space": other}, device_id_type=mesh_id)

    def send_all(buffer, target, c, sent, got):
        @pl.loop(1, spaces)
        def _(offset):
            to_space(buffer, target, c, offset, sent, got).start()

    def all_of(buffer, c, sem):
        span = buffer.at[c, pl.ds(0, spaces - 1)]
        pltpu.make_async_copy(span, span, sem.at[c]).wait()

    for offset in range(1, coils):
        to_coil(state_hbm.at[0:2], seen.at[coil], offset, seen_sent, seen_got).start()

    def clear(row, many):
        for half in range(2):
            halves[half, pl.ds(row, many)] = jnp.zeros((many, unit, lanes), bf16)

    def row_major(g):
        at = pl.ds(pl.multiple_of(g * GROUP, GROUP), GROUP)
        into = pl.ds(g * GROUP + HALO, GROUP)
        for half in range(2):
            for p in range(positions):
                cells = state_ref[half * half_of:(half + 1) * half_of, p, at, :].reshape(half_of * GROUP, width)
                moved = jnp.dot(inward[...], cells, preferred_element_type=f32)
                moved = moved.reshape(GROUP, half_of, width).astype(bf16)
                if lanes > width:
                    moved = jnp.concatenate([moved, jnp.zeros((GROUP, half_of, lanes - width), bf16)], axis=-1)
                halves[half, into, p * half_of:(p + 1) * half_of, :] = moved

    def upright(way, half):
        many = HALO - half
        source, target = (rows + half, HALO)[way], (half, HALO + rows)[way]
        return pltpu.make_async_remote_copy(
            src_ref=halves.at[half, pl.ds(source, many), :, pl.ds(0, wide)],
            dst_ref=halves.at[half, pl.ds(target, many), :, pl.ds(0, wide)],
            send_sem=row_sent.at[way, half], recv_sem=row_got.at[way, half],
            device_id={"space": turn(space, (1, -1)[way], spaces)}, device_id_type=mesh_id)

    wide = -(-width // 128) * 128
    for g in edge_groups:
        fetch_state(g).wait()

    @pl.when(space == 0)
    def _():
        clear(0, HALO)

    @pl.when(space == spaces - 1)
    def _():
        clear(HALO + rows, HALO)

    for unused in (0, 2 * HALO + rows - 1):
        halves[1, unused] = jnp.zeros((unit, lanes), bf16)

    if wide < lanes:
        for first in (0, HALO + rows):
            halves[:, pl.ds(first, HALO), :, wide:lanes] = jnp.zeros((2, HALO, unit, lanes - wide), bf16)
    row_major(0)

    @pl.when(has_above)
    def _():
        for half in range(2):
            upright(1, half).start()

    if groups > 1:
        row_major(groups - 1)

    @pl.when(has_below)
    def _():
        for half in range(2):
            upright(0, half).start()

    fetch_estimate.wait()
    fetch_par.wait()
    for offset in range(1, coils):
        to_coil(state_hbm.at[0:2], seen.at[coil], offset, seen_sent, seen_got).wait()
    for k in range(2):
        whole[k] = jnp.concatenate([seen[j, k].astype(f32).reshape(sites, width) for j in range(coils)], axis=-1)

    @pl.loop(lead, count)
    def _(c):
        fetch_sens(c).start()

    for g in range(1, groups - 1):
        fetch_state(g).start()

    def coil_image(c):
        fetch_sens(c).wait()
        profile_real = sens_ref[0, c].reshape(sites, npar)
        profile_imag = sens_ref[1, c].reshape(sites, npar)
        real = profile_real * whole[0] - profile_imag * whole[1]
        imag = profile_real * whole[1] + profile_imag * whole[0]
        plain = jnp.concatenate([real, imag], axis=0).astype(bf16)
        turned = jnp.concatenate([imag, -real], axis=0).astype(bf16)
        along = (((1,), (1,)), ((), ()))
        spectrum = lax.dot_general(par_ref[0], plain, along, preferred_element_type=f32)
        spectrum += lax.dot_general(par_ref[1], turned, along, preferred_element_type=f32)
        send_out[c] = spectrum.reshape(spaces, held, 2 * sites).astype(bf16)
        got_out[c, space] = send_out[c, space]

    window = min(3, count)

    @pl.loop(0, window)
    def _(c):
        coil_image(c)
        send_all(send_out, got_out, c, out_sent, out_got)

    fetch_pe.start()
    fetch_kdata.start()

    if groups > 2:
        for g in range(1, groups - 1):
            fetch_state(g).wait()

        @pl.loop(1, groups - 1)
        def _(g):
            row_major(g)

    clear(rows + 2 * HALO, deep - rows - 2 * HALO)

    bands = unit * (BLOCK + 2)
    pixel = lax.broadcasted_iota(jnp.int32, (half_of * half_of, bands), 0)
    same_in = pixel % half_of == lax.broadcasted_iota(jnp.int32, (half_of * half_of, bands), 1) % half_of
    outs_of = lax.broadcasted_iota(jnp.int32, (half_of, half_of * half_of), 1) // half_of
    outs_of = jnp.where(outs_of == lax.broadcasted_iota(jnp.int32, outs_of.shape, 0), 1.0, 0.0).astype(bf16)

    @pl.loop(0, layers)
    def _(k):
        taps = kernel_ref[k].reshape(half_of * half_of, 27)
        for c in range(3):
            for po in range(positions):
                chosen = jnp.dot(taps, tap_choice(positions, half_of, bands, po, c), preferred_element_type=f32)
                chosen = jnp.where(same_in, chosen, 0.0).astype(bf16)
                strip[c, po * half_of:(po + 1) * half_of, :] = jnp.dot(outs_of, chosen, preferred_element_type=f32)
        for c in range(3):
            for x in range(BLOCK):
                line = pltpu.roll(strip[c], unit * x, 1) if x else strip[c]
                weight[k, c * BLOCK * unit + unit * x:c * BLOCK * unit + unit * (x + 1), :] = line[:, :bands].astype(bf16)
        own = mixer_ref[k].astype(f32)
        times = positions * BLOCK
        for x in range(times):
            parts_of = [jnp.zeros((half_of, half_of * x), f32)] if x else []
            parts_of.append(own)
            if x < times - 1:
                parts_of.append(jnp.zeros((half_of, half_of * (times - 1 - x)), f32))
            mix[k, half_of * x:half_of * (x + 1), :] = jnp.concatenate(parts_of, axis=-1).astype(bf16)
        offsets = column(bias_ref[pl.ds(k, 1), :], half_of)
        bias[k] = jnp.concatenate([jnp.broadcast_to(offsets, (half_of, 128))] * times, axis=0)

    for half in range(2):
        for g in range(2):
            gains = column(inject_ref[g:g + 1, half * half_of:(half + 1) * half_of], half_of)
            spread[half, g] = jnp.concatenate([jnp.broadcast_to(gains, (half_of, 128))] * positions, axis=0)

    @pl.when(has_below)
    def _():
        for half in range(2):
            upright(0, half).wait_send()
            upright(1, half).wait_recv()

    @pl.when(has_above)
    def _():
        for half in range(2):
            upright(1, half).wait_send()
            upright(0, half).wait_recv()

    lane = lax.broadcasted_iota(jnp.int32, (1, lanes), 1)

    @pl.loop(0, rows + 2 * HALO)
    def _(row):
        for half in range(2):
            line = jnp.where(lane < width, halves[half, row].astype(f32), 0.0)
            strips[0, half, row] = pltpu.roll(line, lanes - width, 1)[:, lanes - 128:].astype(bf16)
            strips[1, half, row] = pltpu.roll(line, width, 1)[:, lanes - 128:].astype(bf16)

    def sideways(way):
        return pltpu.make_async_remote_copy(
            src_ref=strips.at[way], dst_ref=borders.at[way], send_sem=col_sent.at[way], recv_sem=col_got.at[way],
            device_id={"coil": turn(coil, (1, -1)[way], coils)}, device_id_type=mesh_id)

    @pl.when(has_right)
    def _():
        sideways(0).start()

    @pl.when(has_left)
    def _():
        sideways(1).start()

    final = lax.broadcasted_iota(jnp.int32, (1, 128), 1)

    def blend(way, inside):
        @pl.loop(0, rows + 2 * HALO)
        def _(row):
            for half in range(2):
                own = halves[half, row, :, lanes - 128:].astype(f32)
                new = borders[way, half, row].astype(f32)
                halves[half, row, :, lanes - 128:] = jnp.where(inside, new, own).astype(bf16)

    @pl.when(has_left)
    def _():
        sideways(0).wait_recv()
        blend(0, final >= 128 - HALO)

    @pl.when(has_right)
    def _():
        sideways(1).wait_recv()
        first = width % 128
        blend(1, (final >= first) & (final < first + HALO))

    @pl.when(has_right)
    def _():
        sideways(0).wait_send()

    @pl.when(has_left)
    def _():
        sideways(1).wait_send()

    @pl.loop(window, count)
    def _(c):
        coil_image(c)
        all_of(send_out, c - window, out_sent)
        send_all(send_out, got_out, c, out_sent, out_got)

    fetch_pe.wait()
    fetch_kdata.wait()
    pair = max(packed(positions, size, count) for _, size in chunks)
    groups_of = [packed(positions, size, count) for _, size in chunks]

    @pl.loop(0, count // pair)
    def _(couple):
        backs = []
        for j in range(pair):
            c = couple * pair + j
            all_of(got_out, c, out_got)
            blocks = [got_out[c, s].astype(f32) for s in range(spaces)]
            grid = [
                jnp.concatenate([block[:, k * rows:(k + 1) * rows] for block in blocks], axis=-1)
                for k in range(2 * positions)
            ]
            real = jnp.concatenate(grid[:positions], axis=0)
            imag = jnp.concatenate(grid[positions:], axis=0)
            plain = jnp.concatenate([real, imag], axis=0).astype(bf16)
            turned = jnp.concatenate([imag, -real], axis=0).astype(bf16)
            full = jnp.dot(plain, pe_ref[0], preferred_element_type=f32)
            full += jnp.dot(turned, pe_ref[1], preferred_element_type=f32)
            sampled = jnp.concatenate([mask_ref[...].astype(f32)] * positions, axis=0)
            real = sampled * (full[:lines] - kdata_ref[0, c].reshape(lines, npe))
            imag = sampled * (full[lines:] - kdata_ref[1, c].reshape(lines, npe))
            plain = jnp.concatenate([real, imag], axis=0).astype(bf16)
            turned = jnp.concatenate([-imag, real], axis=0).astype(bf16)
            back = jnp.dot(plain, pe_ref[0], preferred_element_type=f32)
            back += jnp.dot(turned, pe_ref[1], preferred_element_type=f32)
            backs.append(back)
            for q, (start, size) in enumerate(chunks):
                many = groups_of[q]
                if (j + 1) % many:
                    continue
                c_group = couple * (pair // many) + j // many
                for s in range(spaces):
                    send_back[q][c_group, s] = jnp.concatenate(
                        [backs[i][k * held:(k + 1) * held, s * rows + start:s * rows + start + size]
                         for i in range(j + 1 - many, j + 1) for k in range(2 * positions)], axis=-1
                    ).astype(bf16)
                got_back[q][c_group, space] = send_back[q][c_group, space]
                if q == 0:
                    send_all(send_back[q], got_back[q], c_group, back_sent[q], back_got[q])

    def release(q):
        sets = count // groups_of[q]

        @pl.loop(0, sets)
        def _(g):
            send_all(send_back[q], got_back[q], g, back_sent[q], back_got[q])

    def drained(q, low, high):
        @pl.loop(low, high)
        def _(g):
            all_of(send_back[q], g, back_sent[q])

    column_at = jnp.where(lane >= lanes - HALO, lane - lanes, lane) + coil * width
    good = (column_at >= 0) & (column_at < total_cols) & ((lane < width + HALO) | (lane >= lanes - HALO))
    column_ok = jnp.where(good, 1.0, 0.0)
    end_ok = column_ok[:, lanes - 128:]

    def extended(value, j):
        after = min(npar, (j + 1) * width + HALO) - j * width
        before = HALO if j else 0
        room = lanes - width
        if j == 0 and lanes <= npar:
            return value[:, :lanes]
        if j == coils - 1 and j * width >= room:
            return jnp.concatenate([value[:, j * width:], value[:, j * width - room:j * width]], axis=-1)
        pieces = [value[:, j * width:j * width + after], jnp.zeros((value.shape[0], lanes - after - before), f32)]
        if before:
            pieces.append(value[:, j * width - before:j * width])
        return jnp.concatenate(pieces, axis=-1)

    def edgeways(way, j):
        return pltpu.make_async_remote_copy(
            src_ref=edge.at[way, j], dst_ref=edges.at[way, coil],
            send_sem=edge_sent.at[way, j], recv_sem=edge_got.at[way, coil],
            device_id={"space": turn(space, (1, -1)[way], spaces), "coil": j}, device_id_type=mesh_id)

    def edge_landed(way):
        for j in range(coils):
            pltpu.make_async_copy(edges.at[way, j], edges.at[way, j], edge_got.at[way, j]).wait()

    def edge_left(way):
        for j in range(coils):
            pltpu.make_async_copy(edge.at[way, j], edge.at[way, j], edge_sent.at[way, j]).wait()

    def limit(value):
        if lanes > 128:
            return jnp.concatenate([value[:, :lanes - 128], value[:, lanes - 128:] * end_ok], axis=-1)
        return value * end_ok

    def merge(row, lines_of):
        spreads = [
            jnp.concatenate([jnp.broadcast_to(lines_of[g][p], (half_of, lanes)) for p in range(positions)], axis=0)
            for g in range(2)
        ]
        for half in range(2):
            gains = [jnp.concatenate([spread[half, g]] * (lanes // 128), axis=-1) for g in range(2)]
            added = gains[0] * spreads[0] + gains[1] * spreads[1]
            halves[half, row] = (halves[half, row].astype(f32) + added).astype(bf16)

    def send_rows(q):
        start, size = chunks[q]
        many = groups_of[q]
        sets = count // many
        spots = positions * size
        at_once = max(1, 256 // (many * 2 * spots))
        while sets % at_once:
            at_once -= 1
        total[:, :spots] = jnp.zeros((2, spots, npar), f32)

        @pl.loop(0, sets // at_once)
        def _(step):
            plains, turneds = [], []
            for i in range(at_once):
                g = step * at_once + i
                all_of(got_back[q], g, back_got[q])
                value = got_back[q][g].astype(f32).reshape(npar, many * 2 * spots)
                plains.append(value)
                for j in range(many):
                    base = j * 2 * spots
                    turneds += [-value[:, base + spots:base + 2 * spots], value[:, base:base + spots]]
            plain = jnp.concatenate(plains, axis=-1).astype(bf16)
            turned = jnp.concatenate(turneds, axis=-1).astype(bf16)
            along = (((0,), (0,)), ((), ()))
            image = lax.dot_general(plain, par_ref[0], along, preferred_element_type=f32)
            image += lax.dot_general(turned, par_ref[1], along, preferred_element_type=f32)
            for i in range(at_once * many):
                c = step * (at_once * many) + i
                base = i * 2 * spots
                real, imag = image[base:base + spots], image[base + spots:base + 2 * spots]
                profile_real = sens_ref[0, c, :, start:start + size, :].reshape(spots, npar)
                profile_imag = sens_ref[1, c, :, start:start + size, :].reshape(spots, npar)
                total[0, :spots] += profile_real * real + profile_imag * imag
                total[1, :spots] += profile_real * imag - profile_imag * real

        for j in range(coils):
            for k in range(2):
                part[q][j, k] = extended(total[k, :spots], j).astype(bf16)
        for offset in range(1, coils):
            to_coil(part[q].at[lax.rem(coil + offset, coils)], parts[q].at[coil], offset, part_sent.at[q], part_got.at[q]).start()
        parts[q][coil] = part[q][coil]

        def put_edge(way, low):
            for j in range(coils):
                edge[way, j] = jnp.concatenate(
                    [extended(total[k, p * size + low:p * size + low + HALO], j) for k in range(2) for p in range(positions)],
                    axis=0).astype(bf16)

            @pl.when((has_below, has_above)[way])
            def _():
                for j in range(coils):
                    edgeways(way, j).start()

        if q == 0:
            put_edge(1, 0)
        if q == len(chunks) - 1:
            put_edge(0, size - HALO)

    def land_rows(q):
        start, size = chunks[q]
        for offset in range(1, coils):
            to_coil(part[q].at[lax.rem(coil + offset, coils)], parts[q].at[coil], offset, part_sent.at[q], part_got.at[q]).wait()
        for k in range(2):
            value = parts[q][0, k].astype(f32)
            for j in range(1, coils):
                value += parts[q][j, k].astype(f32)
            value = limit(value)
            for p in range(positions):
                summed[k, p, start:start + size, :] = value[p * size:(p + 1) * size]

        @pl.loop(start, start + size)
        def _(row):
            merge(row + HALO, [[summed[g, p, pl.ds(row, 1), :] for p in range(positions)] for g in range(2)])

    def merge_border(way):
        first = (0, HALO + rows)[way]
        edge_landed(way)
        value = edges[way, 0].astype(f32)
        for j in range(1, coils):
            value += edges[way, j].astype(f32)
        value = limit(value)
        for r in range(HALO):
            merge(first + r, [
                [value[(g * positions + p) * HALO + r:(g * positions + p) * HALO + r + 1] for p in range(positions)]
                for g in range(2)
            ])

    def cell_rows(layer, blocks):
        source, target = layer % 2, 1 - layer % 2
        high = BLOCK * unit
        news = []
        for row, keep, inner in blocks:
            cells = halves[source, pl.ds(row - 1, BLOCK + 2)].reshape((BLOCK + 2) * unit, lanes)
            taps = jnp.dot(weight[layer], cells, preferred_element_type=f32)
            raw = pltpu.roll(taps[:high], 1, 1) + taps[high:2 * high] + pltpu.roll(taps[2 * high:], lanes - 1, 1)
            hidden = jnp.maximum(raw + jnp.concatenate([bias[layer]] * (lanes // 128), axis=-1), 0.0)
            hidden = limit(hidden)
            if not inner:
                step = lax.broadcasted_iota(jnp.int32, (high, 1), 0) // unit
                at = step + (row - HALO + space * rows)
                hidden = jnp.where((at >= 0) & (at < total_rows), hidden, 0.0)
            update = jnp.dot(mix[layer], hidden.astype(bf16), preferred_element_type=f32)
            if keep < BLOCK:
                update = update[:keep * unit]
            old = halves[target, pl.ds(row, keep)].astype(f32)
            news.append((old + update.reshape(keep, unit, lanes)).astype(bf16))
        for (row, keep, _), new in zip(blocks, news):
            halves[target, pl.ds(row, keep)] = new

    def blocks_of(low, high):
        found = []
        row = low
        while row <= high:
            keep = min(BLOCK, high - row + 1)
            found.append((row + HALO, keep, row >= 0 and row + keep <= rows))
            row += keep
        return found

    def cover(layer, low, high, more=()):
        blocks = blocks_of(low, high)
        blocks += list(more)
        for k in range(0, len(blocks), TOGETHER):
            cell_rows(layer, blocks[k:k + TOGETHER])

    def give(half):
        return pltpu.make_async_copy(
            halves.at[half, pl.ds(HALO, rows), :, pl.ds(0, wide)], state_out.at[half], stage_out.at[half])

    give_gradient = pltpu.make_async_copy(summed.at[:, :, :, pl.ds(0, wide)], gradient_out, summed_out)

    def left_early(q):
        sets = count // groups_of[q]
        return sets * 3 // 4

    def follow(q):
        drained(q, 0, left_early(q))
        release(q + 1)

    done = [layer for layer in range(layers)]
    def couplings(q, which):
        last = q == len(chunks) - 1
        end = sum(chunks[q])
        for layer in which:
            high = end - 2 - layer if not last else rows + HALO - 2 - layer
            cover(layer, done[layer] + 1, high, blocks_of(layer + 1 - HALO, layer) if last else ())
            done[layer] = max(done[layer], high)
            if last and layer >= layers - 2:
                give(1 - layer % 2).start()

    if len(chunks) > 1:
        follow(0)
    send_rows(0)
    land_rows(0)

    @pl.when(has_below)
    def _():
        merge_border(1)

    for q in range(len(chunks) - 1):
        couplings(q, range(layers // 2))
        if q + 2 < len(chunks):
            follow(q + 1)
        send_rows(q + 1)
        couplings(q, range(layers // 2, layers))
        land_rows(q + 1)

    give_gradient.start()

    @pl.when(has_above)
    def _():
        merge_border(0)

    couplings(len(chunks) - 1, range(layers))
    give_gradient.wait()
    for half in range(2):
        give(half).wait()

    @pl.when(has_above)
    def _():
        edge_left(1)

    @pl.when(has_below)
    def _():
        edge_left(0)

    @pl.loop(count - window, count)
    def _(c):
        all_of(send_out, c, out_sent)

    for q in range(len(chunks)):
        drained(q, left_early(q) if q < len(chunks) - 1 else 0, count // groups_of[q])


def finish(half_of, cells_hbm, gradient_hbm, state_out, gradient_out,
           cells_ref, stage, summed, trimmed, outward, cells_in, stage_out, summed_in, summed_out):
    width = state_out.shape[3]
    _, rows, _, wide = cells_hbm.shape
    groups = rows // GROUP

    def fetch(g):
        at = pl.ds(g * GROUP, GROUP)
        return pltpu.make_async_copy(cells_hbm.at[:, at], cells_ref.at[:, at], cells_in.at[g])

    def store(g):
        at = pl.ds(g * GROUP, GROUP)
        return pltpu.make_async_copy(stage.at[:, :, at, :], state_out.at[:, :, at, :], stage_out.at[g])

    fetch_gradient = pltpu.make_async_copy(gradient_hbm, summed, summed_in)
    store_gradient = pltpu.make_async_copy(summed if wide == width else trimmed, gradient_out, summed_out)
    for g in range(groups):
        fetch(g).start()
    fetch_gradient.start()
    outward[...] = swapped(half_of, GROUP)
    for g in range(groups):
        fetch(g).wait()
        for half in range(2):
            for p in range(state_out.shape[1]):
                cells = cells_ref[half, g * GROUP:(g + 1) * GROUP, p * half_of:(p + 1) * half_of, :]
                moved = jnp.dot(outward[...], cells.reshape(GROUP * half_of, wide), preferred_element_type=f32)
                moved = moved[:, :width].reshape(half_of, GROUP, width).astype(bf16)
                stage[half * half_of:(half + 1) * half_of, p, g * GROUP:(g + 1) * GROUP, :] = moved
        store(g).start()
    fetch_gradient.wait()
    if wide != width:
        trimmed[...] = summed[:, :, :, :width]
    store_gradient.start()
    for g in range(groups):
        store(g).wait()
    store_gradient.wait()


def per_device(state, sens, kdata, mask, inject, kernels, biases, mixers):
    spaces, coils = lax.axis_size("space"), lax.axis_size("coil")
    channels, positions, rows, width = state.shape
    count, npar = sens.shape[1], sens.shape[4]
    held, npe = kdata.shape[3:]
    layers, _, outs, _ = kernels.shape
    sites = positions * rows
    unit = positions * outs
    wide = -(-width // 128) * 128
    lanes = -(-(width + 2 * HALO) // 128) * 128
    deep = rows + 2 * HALO + 8
    chunks = row_chunks(rows)
    vmem = pl.BlockSpec(memory_space=pltpu.VMEM)
    hbm = pl.BlockSpec(memory_space=pl.ANY)
    dma = pltpu.SemaphoreType.DMA
    groups = [packed(positions, size, count) for _, size in chunks]
    most = max(size for _, size in chunks)
    backs = [pltpu.VMEM((count // g, spaces, held, g * 2 * positions * size), bf16)
             for g, (_, size) in zip(groups, chunks)]
    shares = [pltpu.VMEM((coils, 2, positions * size, lanes), bf16) for _, size in chunks]
    message = pltpu.VMEM((count, spaces, held, 2 * sites), bf16)
    outer = 2 * positions * HALO
    cells, gradient = pl.pallas_call(
        functools.partial(body, (spaces, coils, rows * spaces, npar, chunks)),
        out_shape=(
            jax.ShapeDtypeStruct((2, rows, unit, wide), bf16),
            jax.ShapeDtypeStruct((2, positions, rows, wide), f32),
        ),
        in_specs=[hbm] * 5 + [vmem] * 5,
        out_specs=(hbm, hbm),
        scratch_shapes=[
            pltpu.VMEM(sens.shape, f32),
            pltpu.VMEM(kdata.shape, f32),
            pltpu.VMEM(state.shape, bf16),
            pltpu.VMEM((2, npar, npar), bf16),
            pltpu.VMEM((2, npe, npe), bf16),
            pltpu.VMEM((coils, 2, positions, rows, width), bf16),
            pltpu.VMEM((2, sites, npar), f32),
            message, message, backs, backs,
            pltpu.VMEM((2, positions * most, npar), f32),
            shares, shares,
            pltpu.VMEM((2, coils, outer, lanes), bf16),
            pltpu.VMEM((2, coils, outer, lanes), bf16),
            pltpu.VMEM((2, deep, unit, lanes), bf16),
            pltpu.VMEM((2, 2, rows + 2 * HALO, unit, 128), bf16),
            pltpu.VMEM((2, 2, rows + 2 * HALO, unit, 128), bf16),
            pltpu.VMEM((layers, 3 * BLOCK * unit, (BLOCK + 2) * unit), bf16),
            pltpu.VMEM((3, unit, (BLOCK + 2) * unit), f32),
            pltpu.VMEM((layers, BLOCK * unit, BLOCK * unit), bf16),
            pltpu.VMEM((layers, BLOCK * unit, 128), f32),
            pltpu.VMEM((2, 2, unit, 128), f32),
            pltpu.VMEM((GROUP * outs, GROUP * outs), bf16),
            pltpu.VMEM((2, positions, rows, lanes), f32),
            dma((count,)), dma, dma((rows // GROUP,)), dma, dma, dma, dma((2,)), dma,
            dma((coils,)), dma((coils,)), dma((count,)), dma((count,)),
            [dma((count // g,)) for g in groups], [dma((count // g,)) for g in groups],
            dma((len(chunks), coils)), dma((len(chunks), coils)), dma((2, coils)), dma((2, coils)),
            dma((2, 2)), dma((2, 2)), dma((2,)), dma((2,)),
        ],
        compiler_params=pltpu.CompilerParams(
            collective_id=0, has_side_effects=True, vmem_limit_bytes=62 * 1024 * 1024),
    )(state, sens, kdata, dft_table(npar), dft_table(npe), mask, inject.T,
      jnp.transpose(kernels, (0, 2, 3, 1)), biases, mixers)
    return pl.pallas_call(
        functools.partial(finish, outs),
        out_shape=(
            jax.ShapeDtypeStruct(state.shape, bf16),
            jax.ShapeDtypeStruct((2, positions, rows, width), f32),
        ),
        in_specs=[hbm] * 2,
        out_specs=(hbm, hbm),
        scratch_shapes=[
            pltpu.VMEM((2, rows, unit, wide), bf16),
            pltpu.VMEM(state.shape, bf16),
            pltpu.VMEM((2, positions, rows, wide), f32),
            pltpu.VMEM((2, positions, rows, width), f32),
            pltpu.VMEM((GROUP * outs, GROUP * outs), bf16),
            dma((rows // GROUP,)), dma((rows // GROUP,)), dma, dma,
        ],
        compiler_params=pltpu.CompilerParams(vmem_limit_bytes=60 * 1024 * 1024),
    )(cells, gradient)


def solution(mesh):
    return jax.shard_map(
        per_device,
        mesh=mesh,
        in_specs=(
            P(None, None, "space", "coil"),
            P(None, "coil", None, "space", None),
            P(None, "coil", None, "space", None),
            P("space", None),
            P(),
            P(),
            P(),
            P(),
        ),
        out_specs=(P(None, None, "space", "coil"), P(None, None, "space", "coil")),
        check_vma=False,
    )
```
